256 devices in a mesh: seq: 64 (over z, y, core), dp: 4 (over x).
Axes of the slice: x: 4, y: 4, z: 8, core: 2. Of those that a mesh axis runs over, the one named last changes fastest.
Arguments:
- queries: bfloat16 [131072, 1024], P(('dp', 'seq')), parts along dimension 0, may hold values from -5 to 5
- key_input: bfloat16 [131072, 128], P(('dp', 'seq')), parts along dimension 0, may hold values from -5 to 5
- value_input: bfloat16 [131072, 128], P(('dp', 'seq')), parts along dimension 0, may hold values from -5 to 5
- attn_out: bfloat16 [131072, 1024], P(('dp', 'seq')), parts along dimension 0, may hold values from -3 to 3
- out_grad: bfloat16 [131072, 1024], P(('dp', 'seq')), parts along dimension 0, may hold values from -5 to 5
- log_norm: float32 [131072, 8], P(('dp', 'seq')), parts along dimension 0, may hold values from 4 to 6
- doc_block: int32 [1024], P('dp'), parts along dimension 0, may hold values from 0 to 127, as said below
Outputs:
- query_grad: bfloat16 [131072, 1024], P(('dp', 'seq')), parts along dimension 0
- key_grad: bfloat16 [131072, 128], P(('dp', 'seq')), parts along dimension 0
- value_grad: bfloat16 [131072, 128], P(('dp', 'seq')), parts along dimension 0
The draws below stay inside these ranges and needn't reach their ends.
There are 4 independent parts, one for each index of `dp`. The reference program is written for one: setup_inputs(seed, part) draws one part's arguments, and reference() takes and returns one part's arrays. A program takes and returns all parts, laid end to end along the dimension named above; each array names one. Nothing has to cross between parts.
Inputs may be any that keep to these rules, and one draw needn't show every extreme that they name: `doc_block`: ids never fall along the sequence and rise by at most one from block to block; every id of 0 to 127 covers 1 to 8 consecutive blocks; id 0 covers exactly the first 8 blocks.
All inputs are finite; a program needn't handle non-finite values.
Results may differ from the reference program's by a relative error of at most 0.0052.
Values may be sent and summed in bfloat16 or wider, within the bound.
No kernel may reach another device: no remote copies, remote signals or barrier semaphores. Data moves between devices by JAX's collectives and lax.ppermute only.
A program may use at most 64 MiB of HBM per device.

```python
import jax
import jax.numpy as jnp
from jax import lax

H = 8
DH = 128
BLK = 128
NBLK = 256
TOKENS = 32768
DOC_MOST = 8
NDOC = 128


def draw_doc_block(key, part):
    rest_docs = NDOC - 1
    extra = NBLK - DOC_MOST - rest_docs
    slot_count = rest_docs * (DOC_MOST - 1)
    order = jax.random.permutation(key, slot_count)
    chosen = (order < extra).astype(jnp.int32)
    counts = jnp.sum(chosen.reshape(rest_docs, DOC_MOST - 1), axis=1)
    lengths = jnp.concatenate([jnp.full((1,), DOC_MOST, jnp.int32), 1 + counts])
    ends = jnp.cumsum(lengths)
    blocks = jnp.arange(NBLK, dtype=jnp.int32)
    return jnp.sum((blocks[:, None] >= ends[None, :]).astype(jnp.int32), axis=1).astype(jnp.int32)


def block_levels(own_key, dims, cuts, low, high):
    def one(position, parts):
        steps = jax.random.uniform(jax.random.fold_in(jax.random.fold_in(own_key, 6), position), (parts,), jnp.float32, low / len(cuts), high / len(cuts))
        return jnp.repeat(jnp.exp(steps), dims[position] // parts).reshape((-1,) + (1,) * (len(dims) - position - 1))

    gain = one(*cuts[0])
    for cut in cuts[1:]:
        gain = gain * one(*cut)
    return gain


def scatter_about(key, shape, deviation, bound, split=(), kind=jnp.bfloat16):
    level = block_levels(key, shape, split, -0.22, 0.18) if split else 1.0
    drawn = jax.random.normal(key, shape, jnp.float32) * deviation * level
    return jnp.minimum(jnp.maximum(drawn, -bound), bound).astype(kind)


def setup_inputs(seed: int = 0, part: int = 0) -> dict:
    keys = jax.random.split(jax.random.key(seed), 8)
    own_keys = jax.random.split(jax.random.fold_in(keys[7], part), 8)
    queries = scatter_about(own_keys[0], (TOKENS, H * DH), 1.0, 5.0, ((0, 64),))
    key_input = scatter_about(own_keys[1], (TOKENS, DH), 1.0, 5.0, ((0, 64),))
    value_input = scatter_about(own_keys[2], (TOKENS, DH), 1.0, 5.0, ((0, 64),))
    attn_out = scatter_about(own_keys[3], (TOKENS, H * DH), 0.5, 3.0, ((0, 64),))
    out_grad = scatter_about(own_keys[4], (TOKENS, H * DH), 1.0, 5.0, ((0, 64),))
    log_norm = jnp.clip(4.0 + 2.0 * jax.random.uniform(own_keys[5], (TOKENS, H), jnp.float32) ** block_levels(own_keys[5], (TOKENS, H), ((0, 64),), -0.2, 0.2), 4.0, 6.0)
    doc_block = draw_doc_block(jax.random.fold_in(jax.random.fold_in(keys[7], part), 71), part)
    return {"queries": queries, "key_input": key_input, "value_input": value_input, "attn_out": attn_out, "out_grad": out_grad, "log_norm": log_norm, "doc_block": doc_block}


def block_terms(query_rows, grad_rows, delta_rows, norm_rows, row_doc, row_pos, key_piece, value_piece, key_doc, key_pos, score_scale):
    contract_last = (((1,), (1,)), ((), ()))
    contract_first = (((0,), (0,)), ((), ()))
    allowed = (row_doc[:, None] == key_doc[None, :]) & (key_pos[None, :] <= row_pos[:, None])
    scores = lax.dot_general(query_rows, key_piece, contract_last, preferred_element_type=jnp.float32) * score_scale
    weights = jnp.where(allowed, jnp.exp(scores - norm_rows[:, None]), jnp.float32(0.0))
    probs_low = weights.astype(jnp.bfloat16)
    prob_grad = lax.dot_general(grad_rows, value_piece, contract_last, preferred_element_type=jnp.float32)
    score_grad = (weights * (prob_grad - delta_rows[:, None])).astype(jnp.bfloat16)
    query_part = jnp.dot(score_grad, key_piece, preferred_element_type=jnp.float32) * score_scale
    key_part = lax.dot_general(score_grad, query_rows, contract_first, preferred_element_type=jnp.float32) * score_scale
    value_part = lax.dot_general(probs_low, grad_rows, contract_first, preferred_element_type=jnp.float32)
    return query_part, key_part, value_part


def reference(queries, key_input, value_input, attn_out, out_grad, log_norm, doc_block):
    tokens, row_width = queries.shape
    head_dim = key_input.shape[1]
    head_count = row_width // head_dim
    score_scale = head_dim ** -0.5
    window = DOC_MOST * BLK
    lead_rows = window - BLK
    block_count = tokens // BLK
    zero_index = jnp.int32(0)
    key_padded = jnp.concatenate([jnp.zeros((lead_rows, head_dim), key_input.dtype), key_input], axis=0)
    value_padded = jnp.concatenate([jnp.zeros((lead_rows, head_dim), value_input.dtype), value_input], axis=0)
    token_doc = jnp.repeat(doc_block, BLK).astype(jnp.int32)
    doc_padded = jnp.concatenate([jnp.full((lead_rows,), -1, jnp.int32), token_doc])
    pos_padded = jnp.arange(tokens + lead_rows, dtype=jnp.int32) - jnp.int32(lead_rows)
    delta_all = jnp.sum(out_grad.reshape(tokens, head_count, head_dim).astype(jnp.float32) * attn_out.reshape(tokens, head_count, head_dim).astype(jnp.float32), axis=-1)

    def one_block(carry, block_index):
        key_acc, value_acc = carry
        start = (block_index * BLK).astype(jnp.int32)
        query_rows = lax.dynamic_slice(queries, (start, zero_index), (BLK, row_width)).reshape(BLK * head_count, head_dim)
        grad_rows = lax.dynamic_slice(out_grad, (start, zero_index), (BLK, row_width)).reshape(BLK * head_count, head_dim)
        delta_rows = lax.dynamic_slice(delta_all, (start, zero_index), (BLK, head_count)).reshape(-1)
        norm_rows = lax.dynamic_slice(log_norm, (start, zero_index), (BLK, head_count)).reshape(-1)
        row_doc = jnp.repeat(lax.dynamic_slice(token_doc, (start,), (BLK,)), head_count)
        row_pos = jnp.repeat(start + jnp.arange(BLK, dtype=jnp.int32), head_count)
        key_piece = lax.dynamic_slice(key_padded, (start, zero_index), (window, head_dim))
        value_piece = lax.dynamic_slice(value_padded, (start, zero_index), (window, head_dim))
        key_doc = lax.dynamic_slice(doc_padded, (start,), (window,))
        key_pos = lax.dynamic_slice(pos_padded, (start,), (window,))
        query_part, key_part, value_part = block_terms(query_rows, grad_rows, delta_rows, norm_rows, row_doc, row_pos, key_piece, value_piece, key_doc, key_pos, score_scale)
        key_acc = lax.dynamic_update_slice(key_acc, lax.dynamic_slice(key_acc, (start, zero_index), (window, head_dim)) + key_part, (start, zero_index))
        value_acc = lax.dynamic_update_slice(value_acc, lax.dynamic_slice(value_acc, (start, zero_index), (window, head_dim)) + value_part, (start, zero_index))
        return (key_acc, value_acc), query_part.astype(jnp.bfloat16)

    empty = jnp.zeros((tokens + lead_rows, head_dim), jnp.float32)
    (key_acc, value_acc), query_blocks = lax.scan(one_block, (empty, empty), jnp.arange(block_count, dtype=jnp.int32))
    query_grad = query_blocks.reshape(tokens, row_width)
    key_grad = key_acc[lead_rows:].astype(jnp.bfloat16)
    value_grad = value_acc[lead_rows:].astype(jnp.bfloat16)
    return (query_grad, key_grad, value_grad)
```

```python
import functools

import jax
import jax.numpy as jnp
from jax import lax
from jax.experimental import pallas as pl
from jax.experimental.pallas import tpu as pltpu
from jax.sharding import PartitionSpec as P

BLK = 128
H = 8
DH = 128
TOK = 512
NB = TOK // BLK
HALF = TOK // 2
LOG2E = 1.4426950408889634
SCALE = DH**-0.5
FAR = -1e30
F32 = jnp.float32
BF16 = jnp.bfloat16
NT = (((1,), (1,)), ((), ()))
NN = (((1,), (0,)), ((), ()))
ANY = pl.BlockSpec(memory_space=pl.ANY)
SMEM = pl.BlockSpec(memory_space=pltpu.SMEM)
VMEM_LIMIT = 48 << 20
HEADS_A = 8


def dot(a, b, dims):
    return lax.dot_general(a, b, dims, preferred_element_type=F32)


def device_index():
    return lax.axis_index("seq")


def own_starts(doc):
    first = device_index() * NB
    starts = [jnp.int32(0)]
    for i in range(1, NB):
        same = doc[first + i] == doc[first + i - 1]
        starts.append(jnp.where(same, starts[-1], jnp.int32(i)))
    return starts


def crossing(doc, distance):
    me = device_index()
    first = me * NB
    key_first = first - NB * distance
    valid = key_first >= 0
    near = jnp.maximum(key_first, 0)
    keys = jnp.int32(0)
    rows = jnp.int32(0)
    for j in range(NB):
        keys += jnp.where(doc[near + j] == doc[first], 1, 0)
        rows += jnp.where(doc[first + j] == doc[near + NB - 1], 1, 0)
    return jnp.where(valid, keys, 0), jnp.where(valid, rows, 0)


def head_cols(h):
    return pl.ds(h * DH, DH)


def copies_in(hbm, buf, sem, heads):
    return [
        pltpu.make_async_copy(hbm.at[:, head_cols(h)], buf.at[n], sem.at[n]) for n, h in enumerate(heads)
    ]


def piece(k, v, k_t, q, g, lnorm, delta, bias):
    s = dot(k, q, NT) * (SCALE * LOG2E) - lnorm
    if bias is not None:
        s = s + bias
    p = jnp.exp2(s)
    ds = (p * (dot(v, g, NT) - delta)).astype(BF16)
    dv = dot(p.astype(BF16), g, NN)
    dk = dot(ds, q, NN)
    dq_t = dot(k_t, ds, NN)
    return dq_t, dk, dv


def fill_bias(doc, bias):
    starts = own_starts(doc)
    key = lax.broadcasted_iota(jnp.int32, (TOK, BLK), 0)
    for i in range(NB):
        tok = lax.broadcasted_iota(jnp.int32, (TOK, BLK), 1) + i * BLK
        ok = (key <= tok) & (key >= starts[i] * BLK)
        bias[:, i * BLK : (i + 1) * BLK] = jnp.where(ok, 0.0, FAR).astype(F32)


def own_head(h, q, g, k, v, k_t, ln, delta, bias, dq_t, dkv, first):
    lnh = ln[h : h + 1, :] * LOG2E
    dlh = delta[h : h + 1, :]
    low = slice(0, HALF)
    high = slice(HALF, TOK)
    x0, dk0, dv0 = piece(k[low, :], v[low, :], k_t[:, low], q, g, lnh, dlh, bias[low, :])
    x1, dk1, dv1 = piece(
        k[high, :], v[high, :], k_t[:, high], q[high, :], g[high, :], lnh[:, high], dlh[:, high], bias[high, high]
    )
    dq_t[:, low] = x0[:, low]
    dq_t[:, high] = x0[:, high] + x1
    for rows, dk, dv in ((low, dk0, dv0), (high, dk1, dv1)):
        if first:
            dkv[rows, 0:DH] = dk
            dkv[rows, DH:] = dv
        else:
            dkv[rows, 0:DH] += dk
            dkv[rows, DH:] += dv


def head_delta(g, a):
    prod = g.astype(F32) * a.astype(F32)
    top = prod.astype(BF16)
    rest = (prod - top.astype(F32)).astype(BF16)
    ones = jnp.ones((8, 2 * DH), BF16)
    both = jnp.concatenate([top, rest], axis=1)
    return dot(ones, both, NT)[0:1, :]


def own_kernel(
    doc, q_hbm, k_hbm, v_hbm, a_hbm, g_hbm, ln_hbm,
    delta_out, dqt_out, dkv_out,
    q, g, a, k, v, k_t, ln, delta, bias, dq_t, dkv, sem_q, sem_g, sem_a, sem_s, sem_o,
):
    heads = list(range(H))
    small = [
        pltpu.make_async_copy(k_hbm, k, sem_s.at[0]),
        pltpu.make_async_copy(v_hbm, v, sem_s.at[1]),
        pltpu.make_async_copy(ln_hbm, ln, sem_s.at[2]),
    ]
    for c in small:
        c.start()
    cq = copies_in(q_hbm, q, sem_q, heads)
    cg = copies_in(g_hbm, g, sem_g, heads)
    ca = copies_in(a_hbm, a, sem_a, heads)
    for h in heads:
        cg[h].start()
        ca[h].start()
        cq[h].start()
    fill_bias(doc, bias)
    for c in small:
        c.wait()
    k_t[...] = jnp.transpose(k[...])
    outs = []
    for h in heads:
        cg[h].wait()
        ca[h].wait()
        cq[h].wait()
        gh = g[h]
        delta[h : h + 1, :] = head_delta(gh, a[h])
        own_head(h, q[h], gh, k, v, k_t, ln, delta, bias, dq_t.at[h], dkv, h == 0)
        c = pltpu.make_async_copy(dq_t.at[h], dqt_out.at[h], sem_o.at[h])
        c.start()
        outs.append(c)
    dkv[:, 0:DH] = dkv[:, 0:DH] * SCALE
    tail = [
        pltpu.make_async_copy(delta, delta_out, sem_s.at[0]),
        pltpu.make_async_copy(dkv, dkv_out, sem_s.at[1]),
    ]
    for c in tail:
        c.start()
    for c in outs + tail:
        c.wait()


def own_pieces(doc, q, k, v, a, g, ln_t):
    big = pltpu.VMEM((H, TOK, DH), BF16)
    return pl.pallas_call(
        own_kernel,
        name="own_pieces",
        out_shape=(
            jax.ShapeDtypeStruct((H, TOK), F32),
            jax.ShapeDtypeStruct((H, DH, TOK), F32),
            jax.ShapeDtypeStruct((TOK, 2 * DH), F32),
        ),
        in_specs=[SMEM] + [ANY] * 6,
        out_specs=(ANY, ANY, ANY),
        scratch_shapes=[
            big, big, big,
            pltpu.VMEM((TOK, DH), BF16),
            pltpu.VMEM((TOK, DH), BF16),
            pltpu.VMEM((DH, TOK), BF16),
            pltpu.VMEM((H, TOK), F32),
            pltpu.VMEM((H, TOK), F32),
            pltpu.VMEM((TOK, TOK), F32),
            pltpu.VMEM((H, DH, TOK), F32),
            pltpu.VMEM((TOK, 2 * DH), F32),
            pltpu.SemaphoreType.DMA((H,)),
            pltpu.SemaphoreType.DMA((H,)),
            pltpu.SemaphoreType.DMA((H,)),
            pltpu.SemaphoreType.DMA((3,)),
            pltpu.SemaphoreType.DMA((H,)),
        ],
        compiler_params=pltpu.CompilerParams(vmem_limit_bytes=VMEM_LIMIT),
        cost_estimate=pl.CostEstimate(flops=4_000_000_000, bytes_accessed=6_000_000, transcendentals=1_600_000),
    )(doc, q, k, v, a, g, ln_t)


def remote_kernel(
    distance, doc, q_hbm, g_hbm, ln_hbm, delta_hbm, kv_hbm,
    dqt_out, kvg_out,
    q, g, kv, k_t, ln, delta, dq_t, acc, kvg, sem_q, sem_g, sem_s, sem_o,
):
    n_keys, n_rows = crossing(doc, distance)

    def run(keys, toks):
        off = TOK - keys
        heads = list(range(H))
        small = [
            pltpu.make_async_copy(kv_hbm, kv, sem_s.at[0]),
            pltpu.make_async_copy(ln_hbm, ln, sem_s.at[1]),
            pltpu.make_async_copy(delta_hbm, delta, sem_s.at[2]),
        ]
        for c in small:
            c.start()
        cq = [
            pltpu.make_async_copy(q_hbm.at[pl.ds(0, toks), head_cols(h)], q.at[h, pl.ds(0, toks)], sem_q.at[h])
            for h in heads
        ]
        cg = [
            pltpu.make_async_copy(g_hbm.at[pl.ds(0, toks), head_cols(h)], g.at[h, pl.ds(0, toks)], sem_g.at[h])
            for h in heads
        ]
        for h in heads:
            cq[h].start()
            cg[h].start()
        for c in small:
            c.wait()
        key_row = lax.broadcasted_iota(jnp.int32, (keys, DH), 0) + off
        live = key_row >= (NB - n_keys) * BLK
        k = jnp.where(live, kv[off:, 0:DH], jnp.zeros((keys, DH), BF16))
        k_t[:, 0:keys] = jnp.transpose(k)
        tok_live = lax.broadcasted_iota(jnp.int32, (H, toks), 1) < n_rows * BLK
        ln[:, 0:toks] = jnp.where(tok_live, ln[:, 0:toks] * LOG2E, -FAR)
        v = kv[off:, DH:]
        outs = []
        for h in heads:
            cq[h].wait()
            cg[h].wait()
            x, dk, dv = piece(
                k, v, k_t[:, 0:keys], q[h, 0:toks, :], g[h, 0:toks, :], ln[h : h + 1, 0:toks], delta[h : h + 1, 0:toks], None
            )
            dq_t[h, :, 0:toks] = x
            if h == 0:
                acc[off:, 0:DH] = dk
                acc[off:, DH:] = dv
            else:
                acc[off:, 0:DH] += dk
                acc[off:, DH:] += dv
            c = pltpu.make_async_copy(dq_t.at[h, :, pl.ds(0, toks)], dqt_out.at[h, :, pl.ds(0, toks)], sem_o.at[h])
            c.start()
            outs.append(c)
        zero = jnp.zeros((keys, DH), F32)
        kvg[off:, 0:DH] = jnp.where(live, acc[off:, 0:DH] * SCALE, zero).astype(BF16)
        kvg[off:, DH:] = jnp.where(live, acc[off:, DH:], zero).astype(BF16)
        if off:
            kvg[0:off, :] = jnp.zeros((off, 2 * DH), BF16)
        for c in outs:
            c.wait()

    few_keys = n_keys * BLK <= HALF
    few_rows = n_rows * BLK <= HALF

    @pl.when(n_keys == 0)
    def _():
        kvg[...] = jnp.zeros((TOK, 2 * DH), BF16)

    for keys in (HALF, TOK):
        for toks in (HALF, TOK):
            ok = (n_keys > 0) & (few_keys == (keys == HALF)) & (few_rows == (toks == HALF))
            pl.when(ok)(functools.partial(run, keys, toks))
    c = pltpu.make_async_copy(kvg, kvg_out, sem_s.at[0])
    c.start()
    c.wait()


def remote_pieces(distance, doc, q, g, ln_t, delta, kv):
    big = pltpu.VMEM((H, TOK, DH), BF16)
    return pl.pallas_call(
        functools.partial(remote_kernel, distance),
        name="remote_pieces",
        out_shape=(
            jax.ShapeDtypeStruct((H, DH, TOK), F32),
            jax.ShapeDtypeStruct((TOK, 2 * DH), BF16),
        ),
        in_specs=[SMEM] + [ANY] * 5,
        out_specs=(ANY, ANY),
        scratch_shapes=[
            big, big,
            pltpu.VMEM((TOK, 2 * DH), BF16),
            pltpu.VMEM((DH, TOK), BF16),
            pltpu.VMEM((H, TOK), F32),
            pltpu.VMEM((H, TOK), F32),
            pltpu.VMEM((H, DH, TOK), F32),
            pltpu.VMEM((TOK, 2 * DH), F32),
            pltpu.VMEM((TOK, 2 * DH), BF16),
            pltpu.SemaphoreType.DMA((H,)),
            pltpu.SemaphoreType.DMA((H,)),
            pltpu.SemaphoreType.DMA((3,)),
            pltpu.SemaphoreType.DMA((H,)),
        ],
        compiler_params=pltpu.CompilerParams(vmem_limit_bytes=VMEM_LIMIT),
        cost_estimate=pl.CostEstimate(flops=4_000_000_000, bytes_accessed=6_000_000, transcendentals=2_000_000),
    )(doc, q, g, ln_t, delta, kv)


def finish_kernel(distances, doc, *refs):
    n = len(distances)
    own_hbm = refs[0]
    rem_hbm = refs[1 : 1 + n]
    dq_out = refs[1 + n]
    own, rem, dq, sem_i, sem_r, sem_o = refs[2 + n :]
    heads = list(range(H))
    ci = [pltpu.make_async_copy(own_hbm.at[h], own.at[h], sem_i.at[h]) for h in heads]
    for c in ci:
        c.start()
    spans = [crossing(doc, d) for d in distances]
    for m, (n_keys, _) in enumerate(spans):

        @pl.when(n_keys > 0)
        def _():
            c = pltpu.make_async_copy(rem_hbm[m], rem.at[m], sem_r.at[m])
            c.start()

    for h in heads:
        ci[h].wait()
    for m, (n_keys, n_rows) in enumerate(spans):

        @pl.when(n_keys > 0)
        def _():
            c = pltpu.make_async_copy(rem_hbm[m], rem.at[m], sem_r.at[m])
            c.wait()
            live = lax.broadcasted_iota(jnp.int32, (DH, TOK), 1) < n_rows * BLK
            for h in heads:
                own[h] += jnp.where(live, rem[m, h], 0.0)

    outs = []
    for h in heads:
        dq[h] = (jnp.transpose(own[h]) * SCALE).astype(BF16)
        c = pltpu.make_async_copy(dq.at[h], dq_out.at[:, head_cols(h)], sem_o.at[h])
        c.start()
        outs.append(c)
    for c in outs:
        c.wait()


def finish_queries(distances, doc, own, rems):
    n = len(distances)
    return pl.pallas_call(
        functools.partial(finish_kernel, distances),
        name="finish_queries",
        out_shape=jax.ShapeDtypeStruct((TOK, H * DH), BF16),
        in_specs=[SMEM] + [ANY] * (1 + n),
        out_specs=ANY,
        scratch_shapes=[
            pltpu.VMEM((H, DH, TOK), F32),
            pltpu.VMEM((n, H, DH, TOK), F32),
            pltpu.VMEM((H, TOK, DH), BF16),
            pltpu.SemaphoreType.DMA((H,)),
            pltpu.SemaphoreType.DMA((n,)),
            pltpu.SemaphoreType.DMA((H,)),
        ],
        compiler_params=pltpu.CompilerParams(vmem_limit_bytes=VMEM_LIMIT),
        cost_estimate=pl.CostEstimate(flops=4_000_000, bytes_accessed=5_000_000, transcendentals=0),
    )(doc, own, *rems)


def moved(value, by):
    count = lax.axis_size("seq")
    return lax.ppermute(value, "seq", [(i, (i + by) % count) for i in range(count)])


def program(distances, queries, key_input, value_input, attn_out, out_grad, log_norm, doc_block):
    ln_t = log_norm.T
    kv = jnp.concatenate([key_input, value_input], axis=1)
    near = [moved(kv, d) for d in distances]
    delta, dqt, dkv = own_pieces(doc_block, queries, key_input, value_input, attn_out, out_grad, ln_t)
    rems = []
    back = []
    for d, part in zip(distances, near):
        dqt_r, kvg = remote_pieces(d, doc_block, queries, out_grad, ln_t, delta, part)
        rems.append(dqt_r)
        back.append(moved(kvg, -d))
    dq = finish_queries(distances, doc_block, dqt, rems)
    for part in back:
        dkv = dkv + part.astype(F32)
    return dq, dkv[:, :DH].astype(BF16), dkv[:, DH:].astype(BF16)


def local(queries, key_input, value_input, attn_out, out_grad, log_norm, doc_block):
    table = doc_block.reshape(-1, NB)
    spans = jnp.any(table[2:, 0] == table[:-2, NB - 1])
    return lax.cond(
        spans,
        functools.partial(program, (1, 2)),
        functools.partial(program, (1,)),
        queries, key_input, value_input, attn_out, out_grad, log_norm, doc_block,
    )


def solution(mesh):
    return jax.shard_map(
        local,
        mesh=mesh,
        in_specs=(
            P(("dp", "seq"), None),
            P(("dp", "seq"), None),
            P(("dp", "seq"), None),
            P(("dp", "seq"), None),
            P(("dp", "seq"), None),
            P(("dp", "seq"), None),
            P("dp"),
        ),
        out_specs=(P(("dp", "seq"), None), P(("dp", "seq"), None), P(("dp", "seq"), None)),
        check_vma=False,
    )
```

```python
import functools

import jax
import jax.numpy as jnp
from jax import lax
from jax.experimental import pallas as pl
from jax.experimental.pallas import tpu as pltpu
from jax.sharding import PartitionSpec as P

BLK = 128
H = 8
DH = 128
TOK = 512
NB = TOK // BLK
HALF = TOK // 2
FAR_TOK = 3 * BLK
LOG2E = 1.4426950408889634
SCALE = DH**-0.5
FAR = -1e30
F32 = jnp.float32
BF16 = jnp.bfloat16
NT = (((1,), (1,)), ((), ()))
NN = (((1,), (0,)), ((), ()))
ANY = pl.BlockSpec(memory_space=pl.ANY)
SMEM = pl.BlockSpec(memory_space=pltpu.SMEM)
VMEM = pl.BlockSpec(memory_space=pltpu.VMEM)
VMEM_LIMIT = 40 << 20
EARLY_LIMIT = 56 << 20
HEADS_A = 4


def dot(a, b, dims):
    return lax.dot_general(a, b, dims, preferred_element_type=F32)


def device_index():
    return lax.axis_index("seq")


def own_starts(doc):
    first = device_index() * NB
    starts = [jnp.int32(0)]
    for i in range(1, NB):
        same = doc[first + i] == doc[first + i - 1]
        starts.append(jnp.where(same, starts[-1], jnp.int32(i)))
    return starts


def crossing(doc, distance):
    me = device_index()
    first = me * NB
    key_first = first - NB * distance
    valid = key_first >= 0
    near = jnp.maximum(key_first, 0)
    keys = jnp.int32(0)
    rows = jnp.int32(0)
    for j in range(NB):
        keys += jnp.where(doc[near + j] == doc[first], 1, 0)
        rows += jnp.where(doc[first + j] == doc[near + NB - 1], 1, 0)
    return jnp.where(valid, keys, 0), jnp.where(valid, rows, 0)


def cols(h):
    return pl.ds(pl.multiple_of(h * DH, DH), DH)


def row(h):
    return pl.ds(h, 1)


def piece(k, v, k_t, q, g, lnorm, delta, bias):
    s = dot(k, q, NT) * (SCALE * LOG2E) - lnorm
    if bias is not None:
        s = s + bias
    p = jnp.exp2(s)
    ds = (p * (dot(v, g, NT) - delta)).astype(BF16)
    dv = dot(p.astype(BF16), g, NN)
    dk = dot(ds, q, NN)
    dq_t = dot(k_t, ds, NN)
    return dq_t, dk, dv


def fill_bias(doc, bias):
    starts = own_starts(doc)
    key = lax.broadcasted_iota(jnp.int32, (TOK, BLK), 0)
    for i in range(NB):
        tok = lax.broadcasted_iota(jnp.int32, (TOK, BLK), 1) + i * BLK
        ok = (key <= tok) & (key >= starts[i] * BLK)
        bias[:, i * BLK : (i + 1) * BLK] = jnp.where(ok, 0.0, FAR).astype(F32)


def own_head(q, g, k, v, k_t, ln, delta, bias, dkv):
    low = slice(0, HALF)
    high = slice(HALF, TOK)
    x0, dk0, dv0 = piece(k[low, :], v[low, :], k_t[:, low], q, g, ln, delta, bias[low, :])
    x1, dk1, dv1 = piece(
        k[high, :], v[high, :], k_t[:, high], q[high, :], g[high, :], ln[:, high], delta[:, high], bias[high, high]
    )
    for rows, dk, dv in ((low, dk0, dv0), (high, dk1, dv1)):
        dkv[rows, 0:DH] += dk
        dkv[rows, DH:] += dv
    return x0[:, low], x0[:, high] + x1


def head_delta(g, a):
    prod = g.astype(F32) * a.astype(F32)
    top = prod.astype(BF16)
    rest = (prod - top.astype(F32)).astype(BF16)
    ones = jnp.ones((8, 2 * DH), BF16)
    return dot(ones, jnp.concatenate([top, rest], axis=1), NT)[0:1, :]


def early_kernel(
    doc, q_hbm, k_hbm, v_hbm, a_hbm, g_hbm, ln_hbm,
    delta_out, dqt_out, dkv_out, far_out,
    q, g, a, k, v, k_t, ln, delta, bias, dq_t, dkv, far, sem_q, sem_g, sem_a, sem_s, sem_o,
):
    small = [
        pltpu.make_async_copy(k_hbm, k, sem_s.at[0]),
        pltpu.make_async_copy(v_hbm, v, sem_s.at[1]),
        pltpu.make_async_copy(ln_hbm, ln, sem_s.at[2]),
    ]

    def copy_q(h):
        return pltpu.make_async_copy(q_hbm.at[:, cols(h)], q.at[h], sem_q.at[h])

    def copy_g(h):
        return pltpu.make_async_copy(g_hbm.at[:, cols(h)], g.at[h], sem_g.at[h])

    def copy_a(h):
        return pltpu.make_async_copy(a_hbm.at[:, cols(h)], a.at[h], sem_a.at[h])

    def copy_o(h):
        return pltpu.make_async_copy(dq_t.at[h], dqt_out.at[h], sem_o.at[h])

    for c in small:
        c.start()
    for h in range(H):
        copy_g(h).start()
        copy_a(h).start()
        if h < HEADS_A:
            copy_q(h).start()
    fill_bias(doc, bias)
    dkv[...] = jnp.zeros((TOK, 2 * DH), F32)
    for c in small:
        c.wait()
    k_t[...] = jnp.transpose(k[...])
    far[:, 0:DH] = k[BLK:, :]
    far[:, DH:] = v[BLK:, :]

    @pl.loop(0, H, unroll=2)
    def _(h):
        copy_g(h).wait()
        copy_a(h).wait()
        delta[row(h), :] = head_delta(g[h], a[h])

    @pl.loop(0, HEADS_A, unroll=2)
    def _(h):
        copy_q(h).wait()
        lo, hi = own_head(q[h], g[h], k, v, k_t, ln[row(h), :] * LOG2E, delta[row(h), :], bias, dkv)
        dq_t[h, :, 0:HALF] = lo
        dq_t[h, :, HALF:] = hi
        copy_o(h).start()

    tail = [
        pltpu.make_async_copy(delta, delta_out, sem_s.at[0]),
        pltpu.make_async_copy(dkv, dkv_out, sem_s.at[1]),
        pltpu.make_async_copy(far, far_out, sem_s.at[2]),
    ]
    for c in tail:
        c.start()
    for h in range(HEADS_A):
        copy_o(h).wait()
    for c in tail:
        c.wait()


def early(doc, q, k, v, a, g, ln_t):
    big = pltpu.VMEM((H, TOK, DH), BF16)
    return pl.pallas_call(
        early_kernel,
        name="early",
        out_shape=(
            jax.ShapeDtypeStruct((H, TOK), F32),
            jax.ShapeDtypeStruct((HEADS_A, DH, TOK), F32),
            jax.ShapeDtypeStruct((TOK, 2 * DH), F32),
            jax.ShapeDtypeStruct((FAR_TOK, 2 * DH), BF16),
        ),
        in_specs=[SMEM] + [ANY] * 6,
        out_specs=(ANY,) * 4,
        scratch_shapes=[
            big, big, big,
            pltpu.VMEM((TOK, DH), BF16),
            pltpu.VMEM((TOK, DH), BF16),
            pltpu.VMEM((DH, TOK), BF16),
            pltpu.VMEM((H, TOK), F32),
            pltpu.VMEM((H, TOK), F32),
            pltpu.VMEM((TOK, TOK), F32),
            pltpu.VMEM((HEADS_A, DH, TOK), F32),
            pltpu.VMEM((TOK, 2 * DH), F32),
            pltpu.VMEM((FAR_TOK, 2 * DH), BF16),
            pltpu.SemaphoreType.DMA((H,)),
            pltpu.SemaphoreType.DMA((H,)),
            pltpu.SemaphoreType.DMA((H,)),
            pltpu.SemaphoreType.DMA((3,)),
            pltpu.SemaphoreType.DMA((H,)),
        ],
        compiler_params=pltpu.CompilerParams(vmem_limit_bytes=EARLY_LIMIT),
        cost_estimate=pl.CostEstimate(flops=4_000_000_000, bytes_accessed=6_000_000, transcendentals=1_600_000),
    )(doc, q, k, v, a, g, ln_t)


def remote_kernel(distance, *refs):
    if distance == 1:
        doc, q, g, ln, delta, k_in, v_in, dqt_out, kvg_out = refs[:9]
        total = TOK
    else:
        doc, q, g, ln, delta, kv_in, dqt_out, kvg_out = refs[:8]
        total = FAR_TOK
    k, k_t, ln2, dq_t, acc, kvg, sem_o, sem_s = refs[-8:]
    n_keys, n_rows = crossing(doc, distance)

    def copy_o(h, toks):
        return pltpu.make_async_copy(dq_t.at[h, :, pl.ds(0, toks)], dqt_out.at[h, :, pl.ds(0, toks)], sem_o.at[h])

    def run(keys, toks):
        off = total - keys
        here = slice(off, total)
        key_row = lax.broadcasted_iota(jnp.int32, (keys, DH), 0)
        live = key_row >= keys - n_keys * BLK
        near = k_in[here, :] if distance == 1 else kv_in[here, 0:DH]
        k[0:keys, :] = jnp.where(live, near, jnp.zeros((keys, DH), BF16))
        k_t[:, 0:keys] = jnp.transpose(k[0:keys, :])
        tok_live = lax.broadcasted_iota(jnp.int32, (H, toks), 1) < n_rows * BLK
        ln2[:, 0:toks] = jnp.where(tok_live, ln[:, 0:toks] * LOG2E, -FAR)
        acc[0:keys, :] = jnp.zeros((keys, 2 * DH), F32)

        @pl.loop(0, H, unroll=2)
        def _(h):
            v = v_in[here, :] if distance == 1 else kv_in[here, DH:]
            x, dk, dv = piece(
                k[0:keys, :], v, k_t[:, 0:keys], q[0:toks, cols(h)], g[0:toks, cols(h)],
                ln2[row(h), 0:toks], delta[row(h), 0:toks], None,
            )
            dq_t[h, :, 0:toks] = x
            acc[0:keys, 0:DH] += dk
            acc[0:keys, DH:] += dv
            copy_o(h, toks).start()

        zero = jnp.zeros((keys, DH), F32)
        kvg[here, 0:DH] = jnp.where(live, acc[0:keys, 0:DH] * SCALE, zero).astype(BF16)
        kvg[here, DH:] = jnp.where(live, acc[0:keys, DH:], zero).astype(BF16)
        if off:
            kvg[0:off, :] = jnp.zeros((off, 2 * DH), BF16)
        for h in range(H):
            copy_o(h, toks).wait()

    few_keys = n_keys * BLK <= HALF
    few_rows = n_rows * BLK <= HALF

    @pl.when(n_keys == 0)
    def _():
        kvg[...] = jnp.zeros((total, 2 * DH), BF16)

    for keys in (HALF, total):
        for toks in (HALF, TOK):
            ok = (n_keys > 0) & (few_keys == (keys == HALF)) & (few_rows == (toks == HALF))
            pl.when(ok)(functools.partial(run, keys, toks))
    c = pltpu.make_async_copy(kvg, kvg_out, sem_s.at[0])
    c.start()
    c.wait()


def remote_pieces(distance, doc, q, g, ln_t, delta, *kv):
    total = TOK if distance == 1 else FAR_TOK
    return pl.pallas_call(
        functools.partial(remote_kernel, distance),
        name=f"remote_{distance}",
        out_shape=(
            jax.ShapeDtypeStruct((H, DH, TOK), F32),
            jax.ShapeDtypeStruct((total, 2 * DH), BF16),
        ),
        in_specs=[SMEM] + [VMEM] * (4 + len(kv)),
        out_specs=(ANY, ANY),
        scratch_shapes=[
            pltpu.VMEM((total, DH), BF16),
            pltpu.VMEM((DH, total), BF16),
            pltpu.VMEM((H, TOK), F32),
            pltpu.VMEM((H, DH, TOK), F32),
            pltpu.VMEM((total, 2 * DH), F32),
            pltpu.VMEM((total, 2 * DH), BF16),
            pltpu.SemaphoreType.DMA((H,)),
            pltpu.SemaphoreType.DMA((1,)),
        ],
        compiler_params=pltpu.CompilerParams(vmem_limit_bytes=VMEM_LIMIT),
        cost_estimate=pl.CostEstimate(flops=4_000_000_000, bytes_accessed=6_000_000, transcendentals=2_000_000),
    )(doc, q, g, ln_t, delta, *kv)


def late_kernel(
    doc, q, k, v, g, ln, delta, own_hbm, rem1_hbm, rem2_hbm,
    dq_out, dkv_out,
    k_t, bias, own, rem1, rem2, dq, dkv, sem_i, sem_r, sem_o,
):
    c_own = pltpu.make_async_copy(own_hbm, own.at[pl.ds(0, HEADS_A)], sem_i.at[0])
    c_own.start()
    spans = [crossing(doc, d) for d in (1, 2)]
    rems = (rem1, rem2)
    copies = [pltpu.make_async_copy(src, dst, sem_r.at[m]) for m, (src, dst) in enumerate(((rem1_hbm, rem1), (rem2_hbm, rem2)))]
    for c, (n_keys, _) in zip(copies, spans):
        pl.when(n_keys > 0)(c.start)
    if HEADS_A < H:
        fill_bias(doc, bias)
        k_t[...] = jnp.transpose(k[...])
        dkv[...] = jnp.zeros((TOK, 2 * DH), F32)

        @pl.loop(HEADS_A, H, unroll=2)
        def _(h):
            lo, hi = own_head(
                q[:, cols(h)], g[:, cols(h)], k, v, k_t, ln[row(h), :] * LOG2E, delta[row(h), :], bias, dkv
            )
            own[h, :, 0:HALF] = lo
            own[h, :, HALF:] = hi

        c_dkv = pltpu.make_async_copy(dkv, dkv_out, sem_i.at[1])
        c_dkv.start()
    c_own.wait()
    for c, rem, (n_keys, n_rows) in zip(copies, rems, spans):

        @pl.when(n_keys > 0)
        def _():
            c.wait()
            live = lax.broadcasted_iota(jnp.int32, (DH, TOK), 1) < n_rows * BLK

            @pl.loop(0, H, unroll=2)
            def _(h):
                own[h] += jnp.where(live, rem[h], 0.0)

    def copy_o(h):
        return pltpu.make_async_copy(dq.at[h], dq_out.at[:, cols(h)], sem_o.at[h])

    @pl.loop(0, H, unroll=2)
    def _(h):
        dq[h] = (jnp.transpose(own[h]) * SCALE).astype(BF16)
        copy_o(h).start()

    for h in range(H):
        copy_o(h).wait()
    if HEADS_A < H:
        c_dkv.wait()


def late(doc, q, k, v, g, ln_t, delta, own, rem1, rem2):
    every = pltpu.VMEM((H, DH, TOK), F32)
    return pl.pallas_call(
        late_kernel,
        name="late",
        out_shape=(
            jax.ShapeDtypeStruct((TOK, H * DH), BF16),
            jax.ShapeDtypeStruct((TOK, 2 * DH), F32),
        ),
        in_specs=[SMEM] + [VMEM] * 6 + [ANY] * 3,
        out_specs=(ANY, ANY),
        scratch_shapes=[
            pltpu.VMEM((DH, TOK), BF16),
            pltpu.VMEM((TOK, TOK), F32),
            every, every, every,
            pltpu.VMEM((H, TOK, DH), BF16),
            pltpu.VMEM((TOK, 2 * DH), F32),
            pltpu.SemaphoreType.DMA((2,)),
            pltpu.SemaphoreType.DMA((2,)),
            pltpu.SemaphoreType.DMA((H,)),
        ],
        compiler_params=pltpu.CompilerParams(vmem_limit_bytes=VMEM_LIMIT),
        cost_estimate=pl.CostEstimate(flops=4_000_000_000, bytes_accessed=5_000_000, transcendentals=0),
    )(doc, q, k, v, g, ln_t, delta, own, rem1, rem2)


def moved(value, by):
    count = lax.axis_size("seq")
    return lax.ppermute(value, "seq", [(i, (i + by) % count) for i in range(count)])


def local(queries, key_input, value_input, attn_out, out_grad, log_norm, doc_block):
    ln_t = log_norm.T
    near_k = moved(key_input, 1)
    near_v = moved(value_input, 1)
    delta, dqt, dkv_a, far = early(doc_block, queries, key_input, value_input, attn_out, out_grad, ln_t)
    far = moved(far, 2)
    rem1, part1 = remote_pieces(1, doc_block, queries, out_grad, ln_t, delta, near_k, near_v)
    back1 = moved(part1, -1)
    rem2, part2 = remote_pieces(2, doc_block, queries, out_grad, ln_t, delta, far)
    back2 = moved(part2, -2)
    dq, dkv_b = late(doc_block, queries, key_input, value_input, out_grad, ln_t, delta, dqt, rem1, rem2)
    dkv = dkv_a + dkv_b
    dk = dkv[:, :DH] * SCALE + back1[:, :DH].astype(F32)
    dv = dkv[:, DH:] + back1[:, DH:].astype(F32)
    dk = jnp.concatenate([dk[:BLK], dk[BLK:] + back2[:, :DH].astype(F32)], axis=0)
    dv = jnp.concatenate([dv[:BLK], dv[BLK:] + back2[:, DH:].astype(F32)], axis=0)
    return dq, dk.astype(BF16), dv.astype(BF16)


def solution(mesh):
    return jax.shard_map(
        local,
        mesh=mesh,
        in_specs=(
            P(("dp", "seq"), None),
            P(("dp", "seq"), None),
            P(("dp", "seq"), None),
            P(("dp", "seq"), None),
            P(("dp", "seq"), None),
            P(("dp", "seq"), None),
            P("dp"),
        ),
        out_specs=(P(("dp", "seq"), None), P(("dp", "seq"), None), P(("dp", "seq"), None)),
        check_vma=False,
    )
```

```python
import functools

import jax
import jax.numpy as jnp
from jax import lax
from jax.experimental import pallas as pl
from jax.experimental.pallas import tpu as pltpu
from jax.sharding import PartitionSpec as P

BLK = 128
H = 8
DH = 128
TOK = 512
NB = TOK // BLK
HALF = TOK // 2
FAR_TOK = 3 * BLK
LOG2E = 1.4426950408889634
SCALE = DH**-0.5
FAR = -1e30
F32 = jnp.float32
BF16 = jnp.bfloat16
NT = (((1,), (1,)), ((), ()))
NN = (((1,), (0,)), ((), ()))
ANY = pl.BlockSpec(memory_space=pl.ANY)
SMEM = pl.BlockSpec(memory_space=pltpu.SMEM)
VMEM = pl.BlockSpec(memory_space=pltpu.VMEM)
VMEM_LIMIT = 40 << 20
EARLY_LIMIT = 56 << 20
HEADS_A = 4


def dot(a, b, dims):
    return lax.dot_general(a, b, dims, preferred_element_type=F32)


def device_index():
    return lax.axis_index("seq")


def own_starts(doc):
    first = device_index() * NB
    starts = [jnp.int32(0)]
    for i in range(1, NB):
        same = doc[first + i] == doc[first + i - 1]
        starts.append(jnp.where(same, starts[-1], jnp.int32(i)))
    return starts


def crossing(doc, distance):
    me = device_index()
    first = me * NB
    key_first = first - NB * distance
    valid = key_first >= 0
    near = jnp.maximum(key_first, 0)
    keys = jnp.int32(0)
    rows = jnp.int32(0)
    for j in range(NB):
        keys += jnp.where(doc[near + j] == doc[first], 1, 0)
        rows += jnp.where(doc[first + j] == doc[near + NB - 1], 1, 0)
    return jnp.where(valid, keys, 0), jnp.where(valid, rows, 0)


def cols(h):
    return pl.ds(pl.multiple_of(h * DH, DH), DH)


def row(h):
    return pl.ds(h, 1)


def piece(k, v, k_t, q, g, lnorm, delta, bias):
    s = dot(k, q, NT) * (SCALE * LOG2E) - lnorm
    if bias is not None:
        s = s + bias
    p = jnp.exp2(s)
    ds = (p * (dot(v, g, NT) - delta)).astype(BF16)
    dv = dot(p.astype(BF16), g, NN)
    dk = dot(ds, q, NN)
    dq_t = dot(k_t, ds, NN)
    return dq_t, dk, dv


def fill_bias(doc, bias):
    starts = own_starts(doc)
    key = lax.broadcasted_iota(jnp.int32, (TOK, BLK), 0)
    for i in range(NB):
        tok = lax.broadcasted_iota(jnp.int32, (TOK, BLK), 1) + i * BLK
        ok = (key <= tok) & (key >= starts[i] * BLK)
        bias[:, i * BLK : (i + 1) * BLK] = jnp.where(ok, 0.0, FAR).astype(F32)


def own_head(q, g, k, v, k_t, ln, delta, bias, dkv):
    low = slice(0, HALF)
    high = slice(HALF, TOK)
    x0, dk0, dv0 = piece(k[low, :], v[low, :], k_t[:, low], q, g, ln, delta, bias[low, :])
    x1, dk1, dv1 = piece(
        k[high, :], v[high, :], k_t[:, high], q[high, :], g[high, :], ln[:, high], delta[:, high], bias[high, high]
    )
    for rows, dk, dv in ((low, dk0, dv0), (high, dk1, dv1)):
        dkv[rows, 0:DH] += dk
        dkv[rows, DH:] += dv
    return x0[:, low], x0[:, high] + x1


def head_delta(g, a):
    prod = g.astype(F32) * a.astype(F32)
    top = prod.astype(BF16)
    rest = (prod - top.astype(F32)).astype(BF16)
    ones = jnp.ones((8, 2 * DH), BF16)
    return dot(ones, jnp.concatenate([top, rest], axis=1), NT)[0:1, :]


def early_kernel(
    doc, q_hbm, k_hbm, v_hbm, a_hbm, g_hbm, ln_hbm,
    delta_out, dqt_out, dkv_out,
    q, g, a, k, v, k_t, ln, delta, bias, dq_t, dkv, sem_q, sem_g, sem_a, sem_s, sem_o,
):
    small = [
        pltpu.make_async_copy(k_hbm, k, sem_s.at[0]),
        pltpu.make_async_copy(v_hbm, v, sem_s.at[1]),
        pltpu.make_async_copy(ln_hbm, ln, sem_s.at[2]),
    ]

    def copy_q(h):
        return pltpu.make_async_copy(q_hbm.at[:, cols(h)], q.at[h], sem_q.at[h])

    def copy_g(h):
        return pltpu.make_async_copy(g_hbm.at[:, cols(h)], g.at[h], sem_g.at[h])

    def copy_a(h):
        return pltpu.make_async_copy(a_hbm.at[:, cols(h)], a.at[h], sem_a.at[h])

    def copy_o(h):
        return pltpu.make_async_copy(dq_t.at[h], dqt_out.at[h], sem_o.at[h])

    for c in small:
        c.start()
    for h in range(H):
        copy_g(h).start()
        copy_a(h).start()
        if h < HEADS_A:
            copy_q(h).start()
    fill_bias(doc, bias)
    dkv[...] = jnp.zeros((TOK, 2 * DH), F32)
    for c in small:
        c.wait()
    k_t[...] = jnp.transpose(k[...])

    @pl.loop(0, H, unroll=2)
    def _(h):
        copy_g(h).wait()
        copy_a(h).wait()
        delta[row(h), :] = head_delta(g[h], a[h])

    @pl.loop(0, HEADS_A, unroll=2)
    def _(h):
        copy_q(h).wait()
        lo, hi = own_head(q[h], g[h], k, v, k_t, ln[row(h), :] * LOG2E, delta[row(h), :], bias, dkv)
        dq_t[h, :, 0:HALF] = lo
        dq_t[h, :, HALF:] = hi
        copy_o(h).start()

    tail = [
        pltpu.make_async_copy(delta, delta_out, sem_s.at[0]),
        pltpu.make_async_copy(dkv, dkv_out, sem_s.at[1]),
    ]
    for c in tail:
        c.start()
    for h in range(HEADS_A):
        copy_o(h).wait()
    for c in tail:
        c.wait()


def early(doc, q, k, v, a, g, ln_t):
    big = pltpu.VMEM((H, TOK, DH), BF16)
    return pl.pallas_call(
        early_kernel,
        name="early",
        out_shape=(
            jax.ShapeDtypeStruct((H, TOK), F32),
            jax.ShapeDtypeStruct((HEADS_A, DH, TOK), F32),
            jax.ShapeDtypeStruct((TOK, 2 * DH), F32),
        ),
        in_specs=[SMEM] + [ANY] * 6,
        out_specs=(ANY,) * 3,
        scratch_shapes=[
            big, big, big,
            pltpu.VMEM((TOK, DH), BF16),
            pltpu.VMEM((TOK, DH), BF16),
            pltpu.VMEM((DH, TOK), BF16),
            pltpu.VMEM((H, TOK), F32),
            pltpu.VMEM((H, TOK), F32),
            pltpu.VMEM((TOK, TOK), F32),
            pltpu.VMEM((HEADS_A, DH, TOK), F32),
            pltpu.VMEM((TOK, 2 * DH), F32),
            pltpu.SemaphoreType.DMA((H,)),
            pltpu.SemaphoreType.DMA((H,)),
            pltpu.SemaphoreType.DMA((H,)),
            pltpu.SemaphoreType.DMA((3,)),
            pltpu.SemaphoreType.DMA((H,)),
        ],
        compiler_params=pltpu.CompilerParams(vmem_limit_bytes=EARLY_LIMIT),
        cost_estimate=pl.CostEstimate(flops=4_000_000_000, bytes_accessed=6_000_000, transcendentals=1_600_000),
    )(doc, q, k, v, a, g, ln_t)


def remote_kernel(
    doc, q, g, ln, delta_hbm, k1, v1, k2, v2,
    dqt_out, near_out, far_out,
    delta, k, k_t, ln2, dq_t, acc, near, far, sem_o, sem_s,
):
    c_delta = pltpu.make_async_copy(delta_hbm, delta, sem_s.at[0])
    c_delta.start()
    n_keys, n_rows = crossing(doc, 1)
    n_far, _ = crossing(doc, 2)

    def copy_o(h, toks):
        return pltpu.make_async_copy(dq_t.at[h, :, pl.ds(0, toks)], dqt_out.at[h, :, pl.ds(0, toks)], sem_o.at[h])

    def mask_rows(toks):
        tok_live = lax.broadcasted_iota(jnp.int32, (H, toks), 1) < n_rows * BLK
        ln2[:, 0:toks] = jnp.where(tok_live, ln[:, 0:toks] * LOG2E, -FAR)

    def load_keys(k_in, v_in, keys, count):
        here = slice(TOK - keys, TOK)
        key_row = lax.broadcasted_iota(jnp.int32, (keys, DH), 0)
        live = key_row >= keys - count * BLK
        k[0:keys, :] = jnp.where(live, k_in[here, :], jnp.zeros((keys, DH), BF16))
        k_t[:, 0:keys] = jnp.transpose(k[0:keys, :])
        acc[0:keys, :] = jnp.zeros((keys, 2 * DH), F32)
        return here, live

    def head(h, v, keys, toks):
        x, dk, dv = piece(
            k[0:keys, :], v, k_t[:, 0:keys], q[0:toks, cols(h)], g[0:toks, cols(h)],
            ln2[row(h), 0:toks], delta[row(h), 0:toks], None,
        )
        acc[0:keys, 0:DH] += dk
        acc[0:keys, DH:] += dv
        return x

    def store_keys(out, keys, total, live):
        zero = jnp.zeros((keys, DH), F32)
        here = slice(total - keys, total)
        out[here, 0:DH] = jnp.where(live, acc[0:keys, 0:DH] * SCALE, zero).astype(BF16)
        out[here, DH:] = jnp.where(live, acc[0:keys, DH:], zero).astype(BF16)
        if keys < total:
            out[0 : total - keys, :] = jnp.zeros((total - keys, 2 * DH), BF16)

    def run(keys, toks):
        here, live = load_keys(k1, v1, keys, n_keys)
        mask_rows(toks)

        @pl.loop(0, H, unroll=2)
        def _(h):
            dq_t[h, :, 0:toks] = head(h, v1[here, :], keys, toks)

        store_keys(near, keys, TOK, live)

    def run_far():
        here, live = load_keys(k2, v2, FAR_TOK, n_far)
        mask_rows(TOK)

        @pl.loop(0, H)
        def _(h):
            x = head(h, v2[here, :], FAR_TOK, TOK)
            tok_live = lax.broadcasted_iota(jnp.int32, (DH, TOK), 1) < n_rows * BLK
            dq_t[h] = jnp.where(tok_live, dq_t[h] + x, 0.0)

        store_keys(far, FAR_TOK, FAR_TOK, live)

    few_keys = n_keys * BLK <= HALF
    few_rows = n_rows * BLK <= HALF

    @pl.when(n_keys == 0)
    def _():
        near[...] = jnp.zeros((TOK, 2 * DH), BF16)

    @pl.when(n_far == 0)
    def _():
        far[...] = jnp.zeros((FAR_TOK, 2 * DH), BF16)

    c_delta.wait()
    for keys in (HALF, TOK):
        for toks in (HALF, TOK):
            ok = (n_keys > 0) & (few_keys == (keys == HALF)) & (few_rows == (toks == HALF))
            pl.when(ok)(functools.partial(run, keys, toks))
    pl.when(n_far > 0)(run_far)
    tail = [
        pltpu.make_async_copy(near, near_out, sem_s.at[0]),
        pltpu.make_async_copy(far, far_out, sem_s.at[1]),
    ]
    for c in tail:
        c.start()
    c_dq = pltpu.make_async_copy(dq_t, dqt_out, sem_o.at[0])

    @pl.when(n_keys > 0)
    def _():
        c_dq.start()
        c_dq.wait()

    for c in tail:
        c.wait()


def remote_pieces(doc, q, g, ln_t, delta, k1, v1, k2, v2):
    return pl.pallas_call(
        remote_kernel,
        name="remote",
        out_shape=(
            jax.ShapeDtypeStruct((H, DH, TOK), F32),
            jax.ShapeDtypeStruct((TOK, 2 * DH), BF16),
            jax.ShapeDtypeStruct((FAR_TOK, 2 * DH), BF16),
        ),
        in_specs=[SMEM] + [VMEM] * 3 + [ANY] + [VMEM] * 4,
        out_specs=(ANY, ANY, ANY),
        scratch_shapes=[
            pltpu.VMEM((H, TOK), F32),
            pltpu.VMEM((TOK, DH), BF16),
            pltpu.VMEM((DH, TOK), BF16),
            pltpu.VMEM((H, TOK), F32),
            pltpu.VMEM((H, DH, TOK), F32),
            pltpu.VMEM((TOK, 2 * DH), F32),
            pltpu.VMEM((TOK, 2 * DH), BF16),
            pltpu.VMEM((FAR_TOK, 2 * DH), BF16),
            pltpu.SemaphoreType.DMA((1,)),
            pltpu.SemaphoreType.DMA((2,)),
        ],
        compiler_params=pltpu.CompilerParams(vmem_limit_bytes=VMEM_LIMIT),
        cost_estimate=pl.CostEstimate(flops=4_000_000_000, bytes_accessed=6_000_000, transcendentals=2_000_000),
    )(doc, q, g, ln_t, delta, k1, v1, k2, v2)


def late_kernel(
    doc, q, k, v, g, ln, delta, own_a, rem,
    dq_out, dkv_out,
    k_t, bias, dq, dkv, sem_s, sem_o,
):
    _, n_rows = crossing(doc, 1)
    fill_bias(doc, bias)
    k_t[...] = jnp.transpose(k[...])
    dkv[...] = jnp.zeros((TOK, 2 * DH), F32)

    def copy_o(h):
        return pltpu.make_async_copy(dq.at[h], dq_out.at[:, cols(h)], sem_o.at[h])

    def finish(h, own):
        live = lax.broadcasted_iota(jnp.int32, (DH, TOK), 1) < n_rows * BLK
        full = own + jnp.where(live, rem[h], 0.0)
        dq[h] = (jnp.transpose(full) * SCALE).astype(BF16)
        copy_o(h).start()

    @pl.loop(HEADS_A, H, unroll=2)
    def _(h):
        lo, hi = own_head(
            q[:, cols(h)], g[:, cols(h)], k, v, k_t, ln[row(h), :] * LOG2E, delta[row(h), :], bias, dkv
        )
        finish(h - HEADS_A, own_a[h - HEADS_A])
        finish(h, jnp.concatenate([lo, hi], axis=1))

    c_dkv = pltpu.make_async_copy(dkv, dkv_out, sem_s.at[0])
    c_dkv.start()
    for h in range(H):
        copy_o(h).wait()
    c_dkv.wait()


def late(doc, q, k, v, g, ln_t, delta, own, rem):
    return pl.pallas_call(
        late_kernel,
        name="late",
        out_shape=(
            jax.ShapeDtypeStruct((TOK, H * DH), BF16),
            jax.ShapeDtypeStruct((TOK, 2 * DH), F32),
        ),
        in_specs=[SMEM] + [VMEM] * 8,
        out_specs=(ANY, ANY),
        scratch_shapes=[
            pltpu.VMEM((DH, TOK), BF16),
            pltpu.VMEM((TOK, TOK), F32),
            pltpu.VMEM((H, TOK, DH), BF16),
            pltpu.VMEM((TOK, 2 * DH), F32),
            pltpu.SemaphoreType.DMA((1,)),
            pltpu.SemaphoreType.DMA((H,)),
        ],
        compiler_params=pltpu.CompilerParams(vmem_limit_bytes=VMEM_LIMIT),
        cost_estimate=pl.CostEstimate(flops=4_000_000_000, bytes_accessed=5_000_000, transcendentals=0),
    )(doc, q, k, v, g, ln_t, delta, own, rem)


def moved(value, by):
    count = lax.axis_size("seq")
    return lax.ppermute(value, "seq", [(i, (i + by) % count) for i in range(count)])


def local(queries, key_input, value_input, attn_out, out_grad, log_norm, doc_block):
    ln_t = log_norm.T
    near_k = moved(key_input, 1)
    near_v = moved(value_input, 1)
    far_k = moved(key_input, 2)
    far_v = moved(value_input, 2)
    delta, dqt, dkv_a = early(doc_block, queries, key_input, value_input, attn_out, out_grad, ln_t)
    rem, part1, part2 = remote_pieces(doc_block, queries, out_grad, ln_t, delta, near_k, near_v, far_k, far_v)
    back1 = moved(part1, -1)
    back2 = moved(part2, -2)
    dq, dkv_b = late(doc_block, queries, key_input, value_input, out_grad, ln_t, delta, dqt, rem)
    dkv = dkv_a + dkv_b
    dk = dkv[:, :DH] * SCALE + back1[:, :DH].astype(F32)
    dv = dkv[:, DH:] + back1[:, DH:].astype(F32)
    dk = jnp.concatenate([dk[:BLK], dk[BLK:] + back2[:, :DH].astype(F32)], axis=0)
    dv = jnp.concatenate([dv[:BLK], dv[BLK:] + back2[:, DH:].astype(F32)], axis=0)
    return dq, dk.astype(BF16), dv.astype(BF16)


def solution(mesh):
    return jax.shard_map(
        local,
        mesh=mesh,
        in_specs=(
            P(("dp", "seq"), None),
            P(("dp", "seq"), None),
            P(("dp", "seq"), None),
            P(("dp", "seq"), None),
            P(("dp", "seq"), None),
            P(("dp", "seq"), None),
            P("dp"),
        ),
        out_specs=(P(("dp", "seq"), None), P(("dp", "seq"), None), P(("dp", "seq"), None)),
        check_vma=False,
    )
```

```python
import functools

import jax
import jax.numpy as jnp
from jax import lax
from jax.experimental import pallas as pl
from jax.experimental.pallas import tpu as pltpu
from jax.sharding import PartitionSpec as P

BLK = 128
H = 8
DH = 128
TOK = 512
NB = TOK // BLK
HALF = TOK // 2
FAR_TOK = 3 * BLK
LOG2E = 1.4426950408889634
SCALE = DH**-0.5
FAR = -1e30
F32 = jnp.float32
BF16 = jnp.bfloat16
NT = (((1,), (1,)), ((), ()))
NN = (((1,), (0,)), ((), ()))
ANY = pl.BlockSpec(memory_space=pl.ANY)
SMEM = pl.BlockSpec(memory_space=pltpu.SMEM)
VMEM = pl.BlockSpec(memory_space=pltpu.VMEM)
VMEM_LIMIT = 40 << 20
EARLY_LIMIT = 56 << 20
HEADS_A = 4


def dot(a, b, dims):
    return lax.dot_general(a, b, dims, preferred_element_type=F32)


def device_index():
    return lax.axis_index("seq")


def own_starts(doc):
    first = device_index() * NB
    starts = [jnp.int32(0)]
    for i in range(1, NB):
        same = doc[first + i] == doc[first + i - 1]
        starts.append(jnp.where(same, starts[-1], jnp.int32(i)))
    return starts


def crossing(doc, distance):
    me = device_index()
    first = me * NB
    key_first = first - NB * distance
    valid = key_first >= 0
    near = jnp.maximum(key_first, 0)
    keys = jnp.int32(0)
    rows = jnp.int32(0)
    for j in range(NB):
        keys += jnp.where(doc[near + j] == doc[first], 1, 0)
        rows += jnp.where(doc[first + j] == doc[near + NB - 1], 1, 0)
    return jnp.where(valid, keys, 0), jnp.where(valid, rows, 0)


def cols(h):
    return pl.ds(pl.multiple_of(h * DH, DH), DH)


def row(h):
    return pl.ds(h, 1)


def piece(k, v, k_t, q, g, lnorm, delta, bias):
    s = dot(k, q, NT) * (SCALE * LOG2E) - lnorm
    if bias is not None:
        s = s + bias
    p = jnp.exp2(s)
    ds = (p * (dot(v, g, NT) - delta)).astype(BF16)
    dv = dot(p.astype(BF16), g, NN)
    dk = dot(ds, q, NN)
    dq_t = dot(k_t, ds, NN)
    return dq_t, dk, dv


def fill_bias(doc, bias):
    starts = own_starts(doc)
    key = lax.broadcasted_iota(jnp.int32, (TOK, BLK), 0)
    for i in range(NB):
        tok = lax.broadcasted_iota(jnp.int32, (TOK, BLK), 1) + i * BLK
        ok = (key <= tok) & (key >= starts[i] * BLK)
        bias[:, i * BLK : (i + 1) * BLK] = jnp.where(ok, 0.0, FAR).astype(F32)


def own_head(q, g, k, v, k_t, ln, delta, bias, dkv):
    low = slice(0, HALF)
    high = slice(HALF, TOK)
    x0, dk0, dv0 = piece(k[low, :], v[low, :], k_t[:, low], q, g, ln, delta, bias[low, :])
    x1, dk1, dv1 = piece(
        k[high, :], v[high, :], k_t[:, high], q[high, :], g[high, :], ln[:, high], delta[:, high], bias[high, high]
    )
    for rows, dk, dv in ((low, dk0, dv0), (high, dk1, dv1)):
        dkv[rows, 0:DH] += dk
        dkv[rows, DH:] += dv
    return x0[:, low], x0[:, high] + x1


def head_delta(g, a):
    prod = g.astype(F32) * a.astype(F32)
    top = prod.astype(BF16)
    rest = (prod - top.astype(F32)).astype(BF16)
    ones = jnp.ones((8, 2 * DH), BF16)
    return dot(ones, jnp.concatenate([top, rest], axis=1), NT)[0:1, :]


def early_kernel(
    doc, q_hbm, k_hbm, v_hbm, a_hbm, g_hbm, ln_hbm,
    delta_out, dqt_out, dkv_out, need_out,
    q, g, a, k, v, k_t, ln, delta, bias, dq_t, dkv, sem_q, sem_g, sem_a, sem_s, sem_o,
):
    small = [
        pltpu.make_async_copy(k_hbm, k, sem_s.at[0]),
        pltpu.make_async_copy(v_hbm, v, sem_s.at[1]),
        pltpu.make_async_copy(ln_hbm, ln, sem_s.at[2]),
    ]

    def copy_q(h):
        return pltpu.make_async_copy(q_hbm.at[:, cols(h)], q.at[h], sem_q.at[h])

    def copy_g(h):
        return pltpu.make_async_copy(g_hbm.at[:, cols(h)], g.at[h], sem_g.at[h])

    def copy_a(h):
        return pltpu.make_async_copy(a_hbm.at[:, cols(h)], a.at[h], sem_a.at[h])

    def copy_o(h):
        return pltpu.make_async_copy(dq_t.at[h], dqt_out.at[h], sem_o.at[h])

    for c in small:
        c.start()
    for h in range(H):
        copy_g(h).start()
        copy_a(h).start()
        if h < HEADS_A:
            copy_q(h).start()
    need = jnp.int32(0)
    for d in range(2, doc.shape[0] // NB):
        need = jnp.where(doc[d * NB] == doc[d * NB - NB - 1], 1, need)
    need_out[0] = need
    fill_bias(doc, bias)
    dkv[...] = jnp.zeros((TOK, 2 * DH), F32)
    for c in small:
        c.wait()
    k_t[...] = jnp.transpose(k[...])

    @pl.loop(0, H, unroll=2)
    def _(h):
        copy_g(h).wait()
        copy_a(h).wait()
        delta[row(h), :] = head_delta(g[h], a[h])

    @pl.loop(0, HEADS_A, unroll=2)
    def _(h):
        copy_q(h).wait()
        lo, hi = own_head(q[h], g[h], k, v, k_t, ln[row(h), :] * LOG2E, delta[row(h), :], bias, dkv)
        dq_t[h, :, 0:HALF] = lo
        dq_t[h, :, HALF:] = hi
        copy_o(h).start()

    tail = [
        pltpu.make_async_copy(delta, delta_out, sem_s.at[0]),
        pltpu.make_async_copy(dkv, dkv_out, sem_s.at[1]),
    ]
    for c in tail:
        c.start()
    for h in range(HEADS_A):
        copy_o(h).wait()
    for c in tail:
        c.wait()


def early(doc, q, k, v, a, g, ln_t):
    big = pltpu.VMEM((H, TOK, DH), BF16)
    return pl.pallas_call(
        early_kernel,
        name="early",
        out_shape=(
            jax.ShapeDtypeStruct((H, TOK), F32),
            jax.ShapeDtypeStruct((HEADS_A, DH, TOK), F32),
            jax.ShapeDtypeStruct((TOK, 2 * DH), F32),
            jax.ShapeDtypeStruct((1,), jnp.int32),
        ),
        in_specs=[SMEM] + [ANY] * 6,
        out_specs=(ANY, ANY, ANY, SMEM),
        scratch_shapes=[
            big, big, big,
            pltpu.VMEM((TOK, DH), BF16),
            pltpu.VMEM((TOK, DH), BF16),
            pltpu.VMEM((DH, TOK), BF16),
            pltpu.VMEM((H, TOK), F32),
            pltpu.VMEM((H, TOK), F32),
            pltpu.VMEM((TOK, TOK), F32),
            pltpu.VMEM((HEADS_A, DH, TOK), F32),
            pltpu.VMEM((TOK, 2 * DH), F32),
            pltpu.SemaphoreType.DMA((H,)),
            pltpu.SemaphoreType.DMA((H,)),
            pltpu.SemaphoreType.DMA((H,)),
            pltpu.SemaphoreType.DMA((3,)),
            pltpu.SemaphoreType.DMA((H,)),
        ],
        compiler_params=pltpu.CompilerParams(vmem_limit_bytes=EARLY_LIMIT),
        cost_estimate=pl.CostEstimate(flops=4_000_000_000, bytes_accessed=6_000_000, transcendentals=1_600_000),
    )(doc, q, k, v, a, g, ln_t)


def dead_rows(ln, n_rows, toks):
    tok_live = lax.broadcasted_iota(jnp.int32, (H, toks), 1) < n_rows * BLK
    return jnp.where(tok_live, ln[:, 0:toks] * LOG2E, -FAR)


def load_keys(k_in, keys, count, k, k_t, acc):
    key_row = lax.broadcasted_iota(jnp.int32, (keys, DH), 0)
    live = key_row >= keys - count * BLK
    k[0:keys, :] = jnp.where(live, k_in[TOK - keys :, :], jnp.zeros((keys, DH), BF16))
    k_t[:, 0:keys] = jnp.transpose(k[0:keys, :])
    acc[0:keys, :] = jnp.zeros((keys, 2 * DH), F32)
    return live


def remote_head(h, q, g, v_in, ln2, delta, k, k_t, acc, keys, toks):
    x, dk, dv = piece(
        k[0:keys, :], v_in[TOK - keys :, :], k_t[:, 0:keys], q[0:toks, cols(h)], g[0:toks, cols(h)],
        ln2[row(h), 0:toks], delta[row(h), 0:toks], None,
    )
    acc[0:keys, 0:DH] += dk
    acc[0:keys, DH:] += dv
    return x


def store_keys(out, acc, keys, live):
    zero = jnp.zeros((keys, DH), F32)
    here = slice(TOK - keys, TOK)
    out[here, 0:DH] = jnp.where(live, acc[0:keys, 0:DH] * SCALE, zero).astype(BF16)
    out[here, DH:] = jnp.where(live, acc[0:keys, DH:], zero).astype(BF16)
    if keys < TOK:
        out[0 : TOK - keys, :] = jnp.zeros((TOK - keys, 2 * DH), BF16)


def near_kernel(
    doc, q, g, ln, delta, k_in, v_in,
    dqt_out, near_out,
    k, k_t, ln2, dq_t, acc, near, sem,
):
    n_keys, n_rows = crossing(doc, 1)

    def run(keys, toks):
        live = load_keys(k_in, keys, n_keys, k, k_t, acc)
        ln2[:, 0:toks] = dead_rows(ln, n_rows, toks)

        @pl.loop(0, H, unroll=2)
        def _(h):
            dq_t[h, :, 0:toks] = remote_head(h, q, g, v_in, ln2, delta, k, k_t, acc, keys, toks)

        store_keys(near, acc, keys, live)

    few_keys = n_keys * BLK <= HALF
    few_rows = n_rows * BLK <= HALF

    @pl.when(n_keys == 0)
    def _():
        near[...] = jnp.zeros((TOK, 2 * DH), BF16)

    for keys in (HALF, TOK):
        for toks in (HALF, TOK):
            ok = (n_keys > 0) & (few_keys == (keys == HALF)) & (few_rows == (toks == HALF))
            pl.when(ok)(functools.partial(run, keys, toks))
    c_near = pltpu.make_async_copy(near, near_out, sem.at[0])
    c_dq = pltpu.make_async_copy(dq_t, dqt_out, sem.at[1])
    c_near.start()

    @pl.when(n_keys > 0)
    def _():
        c_dq.start()
        c_dq.wait()

    c_near.wait()


def remote_scratch():
    return [
        pltpu.VMEM((TOK, DH), BF16),
        pltpu.VMEM((DH, TOK), BF16),
        pltpu.VMEM((H, TOK), F32),
        pltpu.VMEM((H, DH, TOK), F32),
        pltpu.VMEM((TOK, 2 * DH), F32),
        pltpu.VMEM((TOK, 2 * DH), BF16),
        pltpu.SemaphoreType.DMA((2,)),
    ]


def near_pieces(doc, q, g, ln_t, delta, k1, v1):
    return pl.pallas_call(
        near_kernel,
        name="near",
        out_shape=(
            jax.ShapeDtypeStruct((H, DH, TOK), F32),
            jax.ShapeDtypeStruct((TOK, 2 * DH), BF16),
        ),
        in_specs=[SMEM] + [VMEM] * 6,
        out_specs=(ANY, ANY),
        scratch_shapes=remote_scratch(),
        compiler_params=pltpu.CompilerParams(vmem_limit_bytes=VMEM_LIMIT),
        cost_estimate=pl.CostEstimate(flops=4_000_000_000, bytes_accessed=6_000_000, transcendentals=2_000_000),
    )(doc, q, g, ln_t, delta, k1, v1)


def far_kernel(
    doc, q, g, ln, delta, k_in, v_in,
    dq_out, far_out,
    k, k_t, ln2, dq_t, acc, far, sem,
):
    n_keys, n_rows = crossing(doc, 2)
    dq_out[...] = jnp.zeros((TOK, H * DH), F32)
    far[...] = jnp.zeros((TOK, 2 * DH), BF16)

    @pl.when(n_keys > 0)
    def _():
        live = load_keys(k_in, TOK, n_keys, k, k_t, acc)
        ln2[...] = dead_rows(ln, n_rows, TOK)

        @pl.loop(0, H)
        def _(h):
            x = remote_head(h, q, g, v_in, ln2, delta, k, k_t, acc, TOK, TOK)
            dq_out[:, cols(h)] = jnp.transpose(x) * SCALE

        store_keys(far, acc, TOK, live)

    c = pltpu.make_async_copy(far, far_out, sem.at[0])
    c.start()
    c.wait()


def far_pieces(doc, q, g, ln_t, delta, k2, v2):
    return pl.pallas_call(
        far_kernel,
        name="far",
        out_shape=(
            jax.ShapeDtypeStruct((TOK, H * DH), F32),
            jax.ShapeDtypeStruct((TOK, 2 * DH), BF16),
        ),
        in_specs=[SMEM] + [VMEM] * 6,
        out_specs=(VMEM, ANY),
        scratch_shapes=remote_scratch(),
        compiler_params=pltpu.CompilerParams(vmem_limit_bytes=VMEM_LIMIT),
        cost_estimate=pl.CostEstimate(flops=4_000_000_000, bytes_accessed=6_000_000, transcendentals=2_000_000),
    )(doc, q, g, ln_t, delta, k2, v2)


def late_kernel(
    doc, q, k, v, g, ln, delta, own_a, rem,
    dq_out, dkv_out,
    k_t, bias, dq, dkv, sem_s, sem_o,
):
    _, n_rows = crossing(doc, 1)
    fill_bias(doc, bias)
    k_t[...] = jnp.transpose(k[...])
    dkv[...] = jnp.zeros((TOK, 2 * DH), F32)

    def copy_o(h):
        return pltpu.make_async_copy(dq.at[h], dq_out.at[:, cols(h)], sem_o.at[h])

    def finish(h, own):
        live = lax.broadcasted_iota(jnp.int32, (DH, TOK), 1) < n_rows * BLK
        full = own + jnp.where(live, rem[h], 0.0)
        dq[h] = (jnp.transpose(full) * SCALE).astype(BF16)
        copy_o(h).start()

    @pl.loop(HEADS_A, H, unroll=2)
    def _(h):
        lo, hi = own_head(
            q[:, cols(h)], g[:, cols(h)], k, v, k_t, ln[row(h), :] * LOG2E, delta[row(h), :], bias, dkv
        )
        finish(h - HEADS_A, own_a[h - HEADS_A])
        finish(h, jnp.concatenate([lo, hi], axis=1))

    c_dkv = pltpu.make_async_copy(dkv, dkv_out, sem_s.at[0])
    c_dkv.start()
    for h in range(H):
        copy_o(h).wait()
    c_dkv.wait()


def late(doc, q, k, v, g, ln_t, delta, own, rem):
    return pl.pallas_call(
        late_kernel,
        name="late",
        out_shape=(
            jax.ShapeDtypeStruct((TOK, H * DH), BF16),
            jax.ShapeDtypeStruct((TOK, 2 * DH), F32),
        ),
        in_specs=[SMEM] + [VMEM] * 8,
        out_specs=(ANY, ANY),
        scratch_shapes=[
            pltpu.VMEM((DH, TOK), BF16),
            pltpu.VMEM((TOK, TOK), F32),
            pltpu.VMEM((H, TOK, DH), BF16),
            pltpu.VMEM((TOK, 2 * DH), F32),
            pltpu.SemaphoreType.DMA((1,)),
            pltpu.SemaphoreType.DMA((H,)),
        ],
        compiler_params=pltpu.CompilerParams(vmem_limit_bytes=VMEM_LIMIT),
        cost_estimate=pl.CostEstimate(flops=4_000_000_000, bytes_accessed=5_000_000, transcendentals=0),
    )(doc, q, k, v, g, ln_t, delta, own, rem)


def moved(value, by):
    count = lax.axis_size("seq")
    return lax.ppermute(value, "seq", [(i, (i + by) % count) for i in range(count)])


def local(queries, key_input, value_input, attn_out, out_grad, log_norm, doc_block):
    ln_t = log_norm.T
    near_k = moved(key_input, 1)
    near_v = moved(value_input, 1)
    delta, dqt, dkv_a, need = early(doc_block, queries, key_input, value_input, attn_out, out_grad, ln_t)
    rem, part = near_pieces(doc_block, queries, out_grad, ln_t, delta, near_k, near_v)
    back = moved(part, -1)
    dq, dkv_b = late(doc_block, queries, key_input, value_input, out_grad, ln_t, delta, dqt, rem)
    dkv = dkv_a + dkv_b
    dk = dkv[:, :DH] * SCALE + back[:, :DH].astype(F32)
    dv = dkv[:, DH:] + back[:, DH:].astype(F32)

    def far_step(_, grads):
        keys, values, grads = lax.optimization_barrier((key_input, value_input, grads))
        far_k = moved(keys, 2)
        far_v = moved(values, 2)
        dq_far, far_part = far_pieces(doc_block, queries, out_grad, ln_t, delta, far_k, far_v)
        far_back = moved(far_part, -2).astype(F32)
        adds = (dq_far, far_back[:, :DH], far_back[:, DH:])
        return tuple((x.astype(F32) + y).astype(BF16) for x, y in zip(grads, adds))

    return lax.fori_loop(0, need[0], far_step, (dq, dk.astype(BF16), dv.astype(BF16)))


def solution(mesh):
    return jax.shard_map(
        local,
        mesh=mesh,
        in_specs=(
            P(("dp", "seq"), None),
            P(("dp", "seq"), None),
            P(("dp", "seq"), None),
            P(("dp", "seq"), None),
            P(("dp", "seq"), None),
            P(("dp", "seq"), None),
            P("dp"),
        ),
        out_specs=(P(("dp", "seq"), None), P(("dp", "seq"), None), P(("dp", "seq"), None)),
        check_vma=False,
    )
```

```python
import functools

import jax
import jax.numpy as jnp
from jax import lax
from jax.experimental import pallas as pl
from jax.experimental.pallas import tpu as pltpu
from jax.sharding import PartitionSpec as P

BLK = 128
H = 8
DH = 128
TOK = 512
NB = TOK // BLK
HALF = TOK // 2
FAR_TOK = 3 * BLK
LOG2E = 1.4426950408889634
SCALE = DH**-0.5
FAR = -1e30
F32 = jnp.float32
BF16 = jnp.bfloat16
NT = (((1,), (1,)), ((), ()))
NN = (((1,), (0,)), ((), ()))
ANY = pl.BlockSpec(memory_space=pl.ANY)
SMEM = pl.BlockSpec(memory_space=pltpu.SMEM)
VMEM = pl.BlockSpec(memory_space=pltpu.VMEM)
VMEM_LIMIT = 40 << 20
DELTA_LIMIT = 56 << 20
LATE_LIMIT = 40 << 20
HEADS_A = 4


def dot(a, b, dims):
    return lax.dot_general(a, b, dims, preferred_element_type=F32)


def device_index():
    return lax.axis_index("seq")


def own_starts(doc):
    first = device_index() * NB
    starts = [jnp.int32(0)]
    for i in range(1, NB):
        same = doc[first + i] == doc[first + i - 1]
        starts.append(jnp.where(same, starts[-1], jnp.int32(i)))
    return starts


def crossing(doc, distance):
    me = device_index()
    first = me * NB
    key_first = first - NB * distance
    valid = key_first >= 0
    near = jnp.maximum(key_first, 0)
    keys = jnp.int32(0)
    rows = jnp.int32(0)
    for j in range(NB):
        keys += jnp.where(doc[near + j] == doc[first], 1, 0)
        rows += jnp.where(doc[first + j] == doc[near + NB - 1], 1, 0)
    return jnp.where(valid, keys, 0), jnp.where(valid, rows, 0)


def cols(h):
    return pl.ds(pl.multiple_of(h * DH, DH), DH)


def row(h):
    return pl.ds(h, 1)


def piece(k, v, k_t, q, g, lnorm, delta, bias):
    s = dot(k, q, NT) * (SCALE * LOG2E) - lnorm
    if bias is not None:
        s = s + bias
    p = jnp.exp2(s)
    ds = (p * (dot(v, g, NT) - delta)).astype(BF16)
    dv = dot(p.astype(BF16), g, NN)
    dk = dot(ds, q, NN)
    dq_t = dot(k_t, ds, NN)
    return dq_t, dk, dv


def fill_bias(doc, bias):
    starts = own_starts(doc)
    key = lax.broadcasted_iota(jnp.int32, (TOK, BLK), 0)
    for i in range(NB):
        tok = lax.broadcasted_iota(jnp.int32, (TOK, BLK), 1) + i * BLK
        ok = (key <= tok) & (key >= starts[i] * BLK)
        bias[:, i * BLK : (i + 1) * BLK] = jnp.where(ok, 0.0, FAR).astype(F32)


def own_head(q, g, k, v, k_t, ln, delta, bias, dkv):
    low = slice(0, HALF)
    high = slice(HALF, TOK)
    x0, dk0, dv0 = piece(k[low, :], v[low, :], k_t[:, low], q, g, ln, delta, bias[low, :])
    x1, dk1, dv1 = piece(
        k[high, :], v[high, :], k_t[:, high], q[high, :], g[high, :], ln[:, high], delta[:, high], bias[high, high]
    )
    for rows, dk, dv in ((low, dk0, dv0), (high, dk1, dv1)):
        dkv[rows, 0:DH] += dk
        dkv[rows, DH:] += dv
    return x0[:, low], x0[:, high] + x1


def delta_kernel(doc, a_hbm, g_hbm, delta_out, need_out, g, a, delta, sem_g, sem_a, sem_s):
    def copy_g(n):
        return pltpu.make_async_copy(g_hbm.at[pl.ds(n * BLK, BLK), :], g.at[n], sem_g.at[n])

    def copy_a(n):
        return pltpu.make_async_copy(a_hbm.at[pl.ds(n * BLK, BLK), :], a.at[n], sem_a.at[n])

    for n in range(NB):
        copy_g(n).start()
        copy_a(n).start()
    need = jnp.int32(0)
    for d in range(2, doc.shape[0] // NB):
        need = jnp.where(doc[d * NB] == doc[d * NB - NB - 1], 1, need)
    need_out[0] = need
    lane_head = lax.broadcasted_iota(jnp.int32, (H, H * DH), 1) // DH
    pick = (lane_head == lax.broadcasted_iota(jnp.int32, (H, H * DH), 0)).astype(F32).astype(BF16)
    for n in range(NB):
        copy_g(n).wait()
        copy_a(n).wait()
        prod = g[n].astype(F32) * a[n].astype(F32)
        top = prod.astype(BF16)
        rest = (prod - top.astype(F32)).astype(BF16)
        delta[:, n * BLK : (n + 1) * BLK] = dot(pick, top, NT) + dot(pick, rest, NT)

    c = pltpu.make_async_copy(delta, delta_out, sem_s.at[0])
    c.start()
    c.wait()


def head_deltas(doc, a, g):
    big = pltpu.VMEM((NB, BLK, H * DH), BF16)
    return pl.pallas_call(
        delta_kernel,
        name="delta",
        out_shape=(jax.ShapeDtypeStruct((H, TOK), F32), jax.ShapeDtypeStruct((1,), jnp.int32)),
        in_specs=[SMEM, ANY, ANY],
        out_specs=(ANY, SMEM),
        scratch_shapes=[
            big, big,
            pltpu.VMEM((H, TOK), F32),
            pltpu.SemaphoreType.DMA((NB,)),
            pltpu.SemaphoreType.DMA((NB,)),
            pltpu.SemaphoreType.DMA((1,)),
        ],
        compiler_params=pltpu.CompilerParams(vmem_limit_bytes=DELTA_LIMIT),
        cost_estimate=pl.CostEstimate(flops=4_000_000, bytes_accessed=2_000_000, transcendentals=0),
    )(doc, a, g)


def early_kernel(doc, q, k, v, g, ln, delta, dq_t, dkv, k_t, bias):
    fill_bias(doc, bias)
    k_t[...] = jnp.transpose(k[...])
    dkv[...] = jnp.zeros((TOK, 2 * DH), F32)

    @pl.loop(0, HEADS_A, unroll=4)
    def _(h):
        lo, hi = own_head(
            q[:, cols(h)], g[:, cols(h)], k, v, k_t, ln[row(h), :] * LOG2E, delta[row(h), :], bias, dkv
        )
        dq_t[h, :, 0:HALF] = lo
        dq_t[h, :, HALF:] = hi


def early(doc, q, k, v, g, ln_t, delta):
    return pl.pallas_call(
        early_kernel,
        name="early",
        out_shape=(
            jax.ShapeDtypeStruct((HEADS_A, DH, TOK), F32),
            jax.ShapeDtypeStruct((TOK, 2 * DH), F32),
        ),
        in_specs=[SMEM] + [VMEM] * 6,
        out_specs=(VMEM, VMEM),
        scratch_shapes=[
            pltpu.VMEM((DH, TOK), BF16),
            pltpu.VMEM((TOK, TOK), F32),
        ],
        compiler_params=pltpu.CompilerParams(vmem_limit_bytes=VMEM_LIMIT),
        cost_estimate=pl.CostEstimate(flops=4_000_000_000, bytes_accessed=6_000_000, transcendentals=1_600_000),
    )(doc, q, k, v, g, ln_t, delta)


def dead_rows(ln, n_rows, toks):
    tok_live = lax.broadcasted_iota(jnp.int32, (H, toks), 1) < n_rows * BLK
    return jnp.where(tok_live, ln[:, 0:toks] * LOG2E, -FAR)


def load_keys(k_in, keys, count, k, k_t, acc):
    key_row = lax.broadcasted_iota(jnp.int32, (keys, DH), 0)
    live = key_row >= keys - count * BLK
    k[0:keys, :] = jnp.where(live, k_in[TOK - keys :, :], jnp.zeros((keys, DH), BF16))
    k_t[:, 0:keys] = jnp.transpose(k[0:keys, :])
    acc[0:keys, :] = jnp.zeros((keys, 2 * DH), F32)
    return live


def remote_head(h, q, g, v_in, ln2, delta, k, k_t, acc, keys, toks):
    x, dk, dv = piece(
        k[0:keys, :], v_in[TOK - keys :, :], k_t[:, 0:keys], q[0:toks, cols(h)], g[0:toks, cols(h)],
        ln2[row(h), 0:toks], delta[row(h), 0:toks], None,
    )
    acc[0:keys, 0:DH] += dk
    acc[0:keys, DH:] += dv
    return x


def store_keys(out, acc, keys, live):
    zero = jnp.zeros((keys, DH), F32)
    here = slice(TOK - keys, TOK)
    out[here, 0:DH] = jnp.where(live, acc[0:keys, 0:DH] * SCALE, zero).astype(BF16)
    out[here, DH:] = jnp.where(live, acc[0:keys, DH:], zero).astype(BF16)
    if keys < TOK:
        out[0 : TOK - keys, :] = jnp.zeros((TOK - keys, 2 * DH), BF16)


def near_kernel(doc, q, g, ln, delta, k_in, v_in, dq_t, near, k, k_t, ln2, acc):
    n_keys, n_rows = crossing(doc, 1)

    def run(keys, toks):
        live = load_keys(k_in, keys, n_keys, k, k_t, acc)
        ln2[:, 0:toks] = dead_rows(ln, n_rows, toks)

        @pl.loop(0, H, unroll=4)
        def _(h):
            dq_t[h, :, 0:toks] = remote_head(h, q, g, v_in, ln2, delta, k, k_t, acc, keys, toks)

        store_keys(near, acc, keys, live)

    few_keys = n_keys * BLK <= HALF
    few_rows = n_rows * BLK <= HALF

    @pl.when(n_keys == 0)
    def _():
        near[...] = jnp.zeros((TOK, 2 * DH), BF16)

    for keys in (HALF, TOK):
        for toks in (HALF, TOK):
            ok = (n_keys > 0) & (few_keys == (keys == HALF)) & (few_rows == (toks == HALF))
            pl.when(ok)(functools.partial(run, keys, toks))


def remote_scratch():
    return [
        pltpu.VMEM((TOK, DH), BF16),
        pltpu.VMEM((DH, TOK), BF16),
        pltpu.VMEM((H, TOK), F32),
        pltpu.VMEM((TOK, 2 * DH), F32),
    ]


def near_pieces(doc, q, g, ln_t, delta, k1, v1):
    return pl.pallas_call(
        near_kernel,
        name="near",
        out_shape=(
            jax.ShapeDtypeStruct((H, DH, TOK), F32),
            jax.ShapeDtypeStruct((TOK, 2 * DH), BF16),
        ),
        in_specs=[SMEM] + [VMEM] * 6,
        out_specs=(VMEM, VMEM),
        scratch_shapes=remote_scratch(),
        compiler_params=pltpu.CompilerParams(vmem_limit_bytes=VMEM_LIMIT),
        cost_estimate=pl.CostEstimate(flops=4_000_000_000, bytes_accessed=6_000_000, transcendentals=2_000_000),
    )(doc, q, g, ln_t, delta, k1, v1)


def far_kernel(
    doc, q, g, ln, delta, k_in, v_in,
    dq_out, far,
    k, k_t, ln2, acc,
):
    n_keys, n_rows = crossing(doc, 2)
    dq_out[...] = jnp.zeros((TOK, H * DH), F32)
    far[...] = jnp.zeros((TOK, 2 * DH), BF16)

    @pl.when(n_keys > 0)
    def _():
        live = load_keys(k_in, TOK, n_keys, k, k_t, acc)
        ln2[...] = dead_rows(ln, n_rows, TOK)

        @pl.loop(0, H)
        def _(h):
            x = remote_head(h, q, g, v_in, ln2, delta, k, k_t, acc, TOK, TOK)
            dq_out[:, cols(h)] = jnp.transpose(x) * SCALE

        store_keys(far, acc, TOK, live)


def far_pieces(doc, q, g, ln_t, delta, k2, v2):
    return pl.pallas_call(
        far_kernel,
        name="far",
        out_shape=(
            jax.ShapeDtypeStruct((TOK, H * DH), F32),
            jax.ShapeDtypeStruct((TOK, 2 * DH), BF16),
        ),
        in_specs=[SMEM] + [VMEM] * 6,
        out_specs=(VMEM, VMEM),
        scratch_shapes=remote_scratch(),
        compiler_params=pltpu.CompilerParams(vmem_limit_bytes=VMEM_LIMIT),
        cost_estimate=pl.CostEstimate(flops=4_000_000_000, bytes_accessed=6_000_000, transcendentals=2_000_000),
    )(doc, q, g, ln_t, delta, k2, v2)


def late_kernel(doc, q, k, v, g, ln, delta, own_a, rem, dq, dkv, k_t, bias):
    _, n_rows = crossing(doc, 1)
    fill_bias(doc, bias)
    k_t[...] = jnp.transpose(k[...])
    dkv[...] = jnp.zeros((TOK, 2 * DH), F32)

    def finish(h, own):
        live = lax.broadcasted_iota(jnp.int32, (DH, TOK), 1) < n_rows * BLK
        full = own + jnp.where(live, rem[h], 0.0)
        dq[:, cols(h)] = (jnp.transpose(full) * SCALE).astype(BF16)

    @pl.loop(HEADS_A, H, unroll=4)
    def _(h):
        lo, hi = own_head(
            q[:, cols(h)], g[:, cols(h)], k, v, k_t, ln[row(h), :] * LOG2E, delta[row(h), :], bias, dkv
        )
        finish(h - HEADS_A, own_a[h - HEADS_A])
        finish(h, jnp.concatenate([lo, hi], axis=1))


def late(doc, q, k, v, g, ln_t, delta, own, rem):
    return pl.pallas_call(
        late_kernel,
        name="late",
        out_shape=(
            jax.ShapeDtypeStruct((TOK, H * DH), BF16),
            jax.ShapeDtypeStruct((TOK, 2 * DH), F32),
        ),
        in_specs=[SMEM] + [VMEM] * 8,
        out_specs=(VMEM, VMEM),
        scratch_shapes=[
            pltpu.VMEM((DH, TOK), BF16),
            pltpu.VMEM((TOK, TOK), F32),
        ],
        compiler_params=pltpu.CompilerParams(vmem_limit_bytes=LATE_LIMIT),
        cost_estimate=pl.CostEstimate(flops=4_000_000_000, bytes_accessed=5_000_000, transcendentals=0),
    )(doc, q, k, v, g, ln_t, delta, own, rem)


def moved(value, by):
    count = lax.axis_size("seq")
    return lax.ppermute(value, "seq", [(i, (i + by) % count) for i in range(count)])


def local(queries, key_input, value_input, attn_out, out_grad, log_norm, doc_block):
    ln_t = log_norm.T
    delta, need = head_deltas(doc_block, attn_out, out_grad)
    keys, values, delta = lax.optimization_barrier((key_input, value_input, delta))
    near_k = moved(keys, 1)
    near_v = moved(values, 1)
    dqt, dkv_a = early(doc_block, queries, key_input, value_input, out_grad, ln_t, delta)
    rem, part = near_pieces(doc_block, queries, out_grad, ln_t, delta, near_k, near_v)
    back = moved(part, -1)
    dq, dkv_b = late(doc_block, queries, key_input, value_input, out_grad, ln_t, delta, dqt, rem)
    dkv = dkv_a + dkv_b
    dk = dkv[:, :DH] * SCALE + back[:, :DH].astype(F32)
    dv = dkv[:, DH:] + back[:, DH:].astype(F32)

    def far_step(_, grads):
        far_k, far_v, grads = lax.optimization_barrier((key_input, value_input, grads))
        far_k = moved(far_k, 2)
        far_v = moved(far_v, 2)
        dq_far, far_part = far_pieces(doc_block, queries, out_grad, ln_t, delta, far_k, far_v)
        far_back = moved(far_part, -2).astype(F32)
        adds = (dq_far, far_back[:, :DH], far_back[:, DH:])
        return tuple((x.astype(F32) + y).astype(BF16) for x, y in zip(grads, adds))

    return lax.fori_loop(0, need[0], far_step, (dq, dk.astype(BF16), dv.astype(BF16)))


def solution(mesh):
    return jax.shard_map(
        local,
        mesh=mesh,
        in_specs=(
            P(("dp", "seq"), None),
            P(("dp", "seq"), None),
            P(("dp", "seq"), None),
            P(("dp", "seq"), None),
            P(("dp", "seq"), None),
            P(("dp", "seq"), None),
            P("dp"),
        ),
        out_specs=(P(("dp", "seq"), None), P(("dp", "seq"), None), P(("dp", "seq"), None)),
        check_vma=False,
    )
```

```python
import functools

import jax
import jax.numpy as jnp
from jax import lax
from jax.experimental import pallas as pl
from jax.experimental.pallas import tpu as pltpu
from jax.sharding import PartitionSpec as P

BLK = 128
H = 8
DH = 128
TOK = 512
NB = TOK // BLK
HALF = TOK // 2
FAR_TOK = 3 * BLK
LOG2E = 1.4426950408889634
SCALE = DH**-0.5
FAR = -1e30
F32 = jnp.float32
BF16 = jnp.bfloat16
NT = (((1,), (1,)), ((), ()))
NN = (((1,), (0,)), ((), ()))
ANY = pl.BlockSpec(memory_space=pl.ANY)
SMEM = pl.BlockSpec(memory_space=pltpu.SMEM)
VMEM = pl.BlockSpec(memory_space=pltpu.VMEM)
VMEM_LIMIT = 40 << 20
DELTA_LIMIT = 56 << 20
LATE_LIMIT = 40 << 20
HEADS_A = 4


def dot(a, b, dims):
    return lax.dot_general(a, b, dims, preferred_element_type=F32)


def device_index():
    return lax.axis_index("seq")


def own_starts(doc):
    first = device_index() * NB
    starts = [jnp.int32(0)]
    for i in range(1, NB):
        same = doc[first + i] == doc[first + i - 1]
        starts.append(jnp.where(same, starts[-1], jnp.int32(i)))
    return starts


def crossing(doc, distance):
    me = device_index()
    first = me * NB
    key_first = first - NB * distance
    valid = key_first >= 0
    near = jnp.maximum(key_first, 0)
    keys = jnp.int32(0)
    rows = jnp.int32(0)
    for j in range(NB):
        keys += jnp.where(doc[near + j] == doc[first], 1, 0)
        rows += jnp.where(doc[first + j] == doc[near + NB - 1], 1, 0)
    return jnp.where(valid, keys, 0), jnp.where(valid, rows, 0)


def cols(h):
    return pl.ds(pl.multiple_of(h * DH, DH), DH)


def row(h):
    return pl.ds(h, 1)


def piece(k, v, k_t, q, g, lnorm, delta, bias):
    s = dot(k, q, NT) * (SCALE * LOG2E) - lnorm
    if bias is not None:
        s = s + bias
    p = jnp.exp2(s)
    ds = (p * (dot(v, g, NT) - delta)).astype(BF16)
    dv = dot(p.astype(BF16), g, NN)
    dk = dot(ds, q, NN)
    dq_t = dot(k_t, ds, NN)
    return dq_t, dk, dv


def fill_bias(doc, bias):
    starts = own_starts(doc)
    key = lax.broadcasted_iota(jnp.int32, (TOK, BLK), 0)
    for i in range(NB):
        tok = lax.broadcasted_iota(jnp.int32, (TOK, BLK), 1) + i * BLK
        ok = (key <= tok) & (key >= starts[i] * BLK)
        bias[:, i * BLK : (i + 1) * BLK] = jnp.where(ok, 0.0, FAR).astype(F32)


def own_head(q, g, k, v, k_t, ln, delta, bias, dkv):
    low = slice(0, HALF)
    high = slice(HALF, TOK)
    x0, dk0, dv0 = piece(k[low, :], v[low, :], k_t[:, low], q, g, ln, delta, bias[low, :])
    x1, dk1, dv1 = piece(
        k[high, :], v[high, :], k_t[:, high], q[high, :], g[high, :], ln[:, high], delta[:, high], bias[high, high]
    )
    for rows, dk, dv in ((low, dk0, dv0), (high, dk1, dv1)):
        dkv[rows, 0:DH] += dk
        dkv[rows, DH:] += dv
    return x0[:, low], x0[:, high] + x1


def delta_kernel(doc, a_hbm, g_hbm, delta_out, need_out, g, a, delta, sem_g, sem_a, sem_s):
    def copy_g(n):
        return pltpu.make_async_copy(g_hbm.at[pl.ds(n * BLK, BLK), :], g.at[n], sem_g.at[n])

    def copy_a(n):
        return pltpu.make_async_copy(a_hbm.at[pl.ds(n * BLK, BLK), :], a.at[n], sem_a.at[n])

    for n in range(NB):
        copy_g(n).start()
        copy_a(n).start()
    need = jnp.int32(0)
    for d in range(2, doc.shape[0] // NB):
        need = jnp.where(doc[d * NB] == doc[d * NB - NB - 1], 1, need)
    need_out[0] = need
    lane_head = lax.broadcasted_iota(jnp.int32, (H, H * DH), 1) // DH
    pick = (lane_head == lax.broadcasted_iota(jnp.int32, (H, H * DH), 0)).astype(F32).astype(BF16)
    for n in range(NB):
        copy_g(n).wait()
        copy_a(n).wait()
        prod = g[n].astype(F32) * a[n].astype(F32)
        top = prod.astype(BF16)
        rest = (prod - top.astype(F32)).astype(BF16)
        delta[:, n * BLK : (n + 1) * BLK] = dot(pick, top, NT) + dot(pick, rest, NT)

    c = pltpu.make_async_copy(delta, delta_out, sem_s.at[0])
    c.start()
    c.wait()


def head_deltas(doc, a, g):
    big = pltpu.VMEM((NB, BLK, H * DH), BF16)
    return pl.pallas_call(
        delta_kernel,
        name="delta",
        out_shape=(jax.ShapeDtypeStruct((H, TOK), F32), jax.ShapeDtypeStruct((1,), jnp.int32)),
        in_specs=[SMEM, ANY, ANY],
        out_specs=(ANY, SMEM),
        scratch_shapes=[
            big, big,
            pltpu.VMEM((H, TOK), F32),
            pltpu.SemaphoreType.DMA((NB,)),
            pltpu.SemaphoreType.DMA((NB,)),
            pltpu.SemaphoreType.DMA((1,)),
        ],
        compiler_params=pltpu.CompilerParams(vmem_limit_bytes=DELTA_LIMIT),
        cost_estimate=pl.CostEstimate(flops=4_000_000, bytes_accessed=2_000_000, transcendentals=0),
    )(doc, a, g)


def early_kernel(doc, q, k, v, g, ln, delta, dq_t, dkv, k_t, bias):
    fill_bias(doc, bias)
    k_t[...] = jnp.transpose(k[...])
    dkv[...] = jnp.zeros((TOK, 2 * DH), F32)

    @pl.loop(0, HEADS_A, unroll=4)
    def _(h):
        lo, hi = own_head(
            q[:, cols(h)], g[:, cols(h)], k, v, k_t, ln[row(h), :] * LOG2E, delta[row(h), :], bias, dkv
        )
        dq_t[h, :, 0:HALF] = lo
        dq_t[h, :, HALF:] = hi


def early(doc, q, k, v, g, ln_t, delta):
    return pl.pallas_call(
        early_kernel,
        name="early",
        out_shape=(
            jax.ShapeDtypeStruct((HEADS_A, DH, TOK), F32),
            jax.ShapeDtypeStruct((TOK, 2 * DH), F32),
        ),
        in_specs=[SMEM] + [VMEM] * 6,
        out_specs=(VMEM, VMEM),
        scratch_shapes=[
            pltpu.VMEM((DH, TOK), BF16),
            pltpu.VMEM((TOK, TOK), F32),
        ],
        compiler_params=pltpu.CompilerParams(vmem_limit_bytes=VMEM_LIMIT),
        cost_estimate=pl.CostEstimate(flops=4_000_000_000, bytes_accessed=6_000_000, transcendentals=1_600_000),
    )(doc, q, k, v, g, ln_t, delta)


def dead_rows(ln, n_rows, toks):
    tok_live = lax.broadcasted_iota(jnp.int32, (H, toks), 1) < n_rows * BLK
    return jnp.where(tok_live, ln[:, 0:toks] * LOG2E, -FAR)


def load_keys(k_in, keys, count, k, k_t, acc):
    key_row = lax.broadcasted_iota(jnp.int32, (keys, DH), 0)
    live = key_row >= keys - count * BLK
    k[0:keys, :] = jnp.where(live, k_in[TOK - keys :, :], jnp.zeros((keys, DH), BF16))
    k_t[:, 0:keys] = jnp.transpose(k[0:keys, :])
    acc[0:keys, :] = jnp.zeros((keys, 2 * DH), F32)
    return live


def remote_head(h, q, g, v_in, ln2, delta, k, k_t, acc, keys, toks):
    x, dk, dv = piece(
        k[0:keys, :], v_in[TOK - keys :, :], k_t[:, 0:keys], q[0:toks, cols(h)], g[0:toks, cols(h)],
        ln2[row(h), 0:toks], delta[row(h), 0:toks], None,
    )
    acc[0:keys, 0:DH] += dk
    acc[0:keys, DH:] += dv
    return x


def store_keys(out, acc, keys, live):
    zero = jnp.zeros((keys, DH), F32)
    here = slice(TOK - keys, TOK)
    out[here, 0:DH] = jnp.where(live, acc[0:keys, 0:DH] * SCALE, zero).astype(BF16)
    out[here, DH:] = jnp.where(live, acc[0:keys, DH:], zero).astype(BF16)
    if keys < TOK:
        out[0 : TOK - keys, :] = jnp.zeros((TOK - keys, 2 * DH), BF16)


def near_kernel(doc, q, g, ln, delta, k_in, v_in, dq_t, near, k, k_t, ln2, acc):
    n_keys, n_rows = crossing(doc, 1)

    def run(keys, toks):
        live = load_keys(k_in, keys, n_keys, k, k_t, acc)
        ln2[:, 0:toks] = dead_rows(ln, n_rows, toks)

        @pl.loop(0, H, unroll=4)
        def _(h):
            dq_t[h, :, 0:toks] = remote_head(h, q, g, v_in, ln2, delta, k, k_t, acc, keys, toks)

        store_keys(near, acc, keys, live)

    few_keys = n_keys * BLK <= HALF
    few_rows = n_rows * BLK <= HALF

    @pl.when(n_keys == 0)
    def _():
        near[...] = jnp.zeros((TOK, 2 * DH), BF16)

    for keys in (HALF, TOK):
        for toks in (HALF, TOK):
            ok = (n_keys > 0) & (few_keys == (keys == HALF)) & (few_rows == (toks == HALF))
            pl.when(ok)(functools.partial(run, keys, toks))


def remote_scratch():
    return [
        pltpu.VMEM((TOK, DH), BF16),
        pltpu.VMEM((DH, TOK), BF16),
        pltpu.VMEM((H, TOK), F32),
        pltpu.VMEM((TOK, 2 * DH), F32),
    ]


def near_pieces(doc, q, g, ln_t, delta, k1, v1):
    return pl.pallas_call(
        near_kernel,
        name="near",
        out_shape=(
            jax.ShapeDtypeStruct((H, DH, TOK), F32),
            jax.ShapeDtypeStruct((TOK, 2 * DH), BF16),
        ),
        in_specs=[SMEM] + [VMEM] * 6,
        out_specs=(VMEM, VMEM),
        scratch_shapes=remote_scratch(),
        compiler_params=pltpu.CompilerParams(vmem_limit_bytes=VMEM_LIMIT),
        cost_estimate=pl.CostEstimate(flops=4_000_000_000, bytes_accessed=6_000_000, transcendentals=2_000_000),
    )(doc, q, g, ln_t, delta, k1, v1)


def far_kernel(
    doc, q, g, ln, delta, k_in, v_in,
    dq_out, far,
    k, k_t, ln2, acc,
):
    n_keys, n_rows = crossing(doc, 2)
    dq_out[...] = jnp.zeros((TOK, H * DH), F32)
    far[...] = jnp.zeros((TOK, 2 * DH), BF16)

    @pl.when(n_keys > 0)
    def _():
        live = load_keys(k_in, TOK, n_keys, k, k_t, acc)
        ln2[...] = dead_rows(ln, n_rows, TOK)

        @pl.loop(0, H)
        def _(h):
            x = remote_head(h, q, g, v_in, ln2, delta, k, k_t, acc, TOK, TOK)
            dq_out[:, cols(h)] = jnp.transpose(x) * SCALE

        store_keys(far, acc, TOK, live)


def far_pieces(doc, q, g, ln_t, delta, k2, v2):
    return pl.pallas_call(
        far_kernel,
        name="far",
        out_shape=(
            jax.ShapeDtypeStruct((TOK, H * DH), F32),
            jax.ShapeDtypeStruct((TOK, 2 * DH), BF16),
        ),
        in_specs=[SMEM] + [VMEM] * 6,
        out_specs=(VMEM, VMEM),
        scratch_shapes=remote_scratch(),
        compiler_params=pltpu.CompilerParams(vmem_limit_bytes=VMEM_LIMIT),
        cost_estimate=pl.CostEstimate(flops=4_000_000_000, bytes_accessed=6_000_000, transcendentals=2_000_000),
    )(doc, q, g, ln_t, delta, k2, v2)


def late_kernel(doc, q, k, v, g, ln, delta, own_a, rem, dq, dkv, k_t, bias):
    _, n_rows = crossing(doc, 1)
    fill_bias(doc, bias)
    k_t[...] = jnp.transpose(k[...])
    dkv[...] = jnp.zeros((TOK, 2 * DH), F32)

    def finish(h, own):
        live = lax.broadcasted_iota(jnp.int32, (DH, TOK), 1) < n_rows * BLK
        full = own + jnp.where(live, rem[h], 0.0)
        dq[:, cols(h)] = (jnp.transpose(full) * SCALE).astype(BF16)

    @pl.loop(HEADS_A, H, unroll=4)
    def _(h):
        lo, hi = own_head(
            q[:, cols(h)], g[:, cols(h)], k, v, k_t, ln[row(h), :] * LOG2E, delta[row(h), :], bias, dkv
        )
        finish(h - HEADS_A, own_a[h - HEADS_A])
        finish(h, jnp.concatenate([lo, hi], axis=1))


def late(doc, q, k, v, g, ln_t, delta, own, rem):
    return pl.pallas_call(
        late_kernel,
        name="late",
        out_shape=(
            jax.ShapeDtypeStruct((TOK, H * DH), BF16),
            jax.ShapeDtypeStruct((TOK, 2 * DH), F32),
        ),
        in_specs=[SMEM] + [VMEM] * 8,
        out_specs=(VMEM, VMEM),
        scratch_shapes=[
            pltpu.VMEM((DH, TOK), BF16),
            pltpu.VMEM((TOK, TOK), F32),
        ],
        compiler_params=pltpu.CompilerParams(vmem_limit_bytes=LATE_LIMIT),
        cost_estimate=pl.CostEstimate(flops=4_000_000_000, bytes_accessed=5_000_000, transcendentals=0),
    )(doc, q, k, v, g, ln_t, delta, own, rem)


def moved(value, by):
    count = lax.axis_size("seq")
    return lax.ppermute(value, "seq", [(i, (i + by) % count) for i in range(count)])


def local(queries, key_input, value_input, attn_out, out_grad, log_norm, doc_block):
    ln_t = log_norm.T
    near_k = moved(key_input, 1)
    near_v = moved(value_input, 1)
    delta, need = head_deltas(doc_block, attn_out, out_grad)
    dqt, dkv_a = early(doc_block, queries, key_input, value_input, out_grad, ln_t, delta)
    rem, part = near_pieces(doc_block, queries, out_grad, ln_t, delta, near_k, near_v)
    back = moved(part, -1)
    dq, dkv_b = late(doc_block, queries, key_input, value_input, out_grad, ln_t, delta, dqt, rem)
    dkv = dkv_a + dkv_b
    dk = dkv[:, :DH] * SCALE + back[:, :DH].astype(F32)
    dv = dkv[:, DH:] + back[:, DH:].astype(F32)

    def far_step(_, grads):
        far_k, far_v, grads = lax.optimization_barrier((key_input, value_input, grads))
        far_k = moved(far_k, 2)
        far_v = moved(far_v, 2)
        dq_far, far_part = far_pieces(doc_block, queries, out_grad, ln_t, delta, far_k, far_v)
        far_back = moved(far_part, -2).astype(F32)
        adds = (dq_far, far_back[:, :DH], far_back[:, DH:])
        return tuple((x.astype(F32) + y).astype(BF16) for x, y in zip(grads, adds))

    return lax.fori_loop(0, need[0], far_step, (dq, dk.astype(BF16), dv.astype(BF16)))


def solution(mesh):
    return jax.shard_map(
        local,
        mesh=mesh,
        in_specs=(
            P(("dp", "seq"), None),
            P(("dp", "seq"), None),
            P(("dp", "seq"), None),
            P(("dp", "seq"), None),
            P(("dp", "seq"), None),
            P(("dp", "seq"), None),
            P("dp"),
        ),
        out_specs=(P(("dp", "seq"), None), P(("dp", "seq"), None), P(("dp", "seq"), None)),
        check_vma=False,
    )
```

```python
import functools

import jax
import jax.numpy as jnp
from jax import lax
from jax.experimental import pallas as pl
from jax.experimental.pallas import tpu as pltpu
from jax.sharding import PartitionSpec as P

BLK = 128
H = 8
DH = 128
TOK = 512
NB = TOK // BLK
HALF = TOK // 2
FAR_TOK = 3 * BLK
LOG2E = 1.4426950408889634
SCALE = DH**-0.5
FAR = -1e30
F32 = jnp.float32
BF16 = jnp.bfloat16
NT = (((1,), (1,)), ((), ()))
NN = (((1,), (0,)), ((), ()))
ANY = pl.BlockSpec(memory_space=pl.ANY)
SMEM = pl.BlockSpec(memory_space=pltpu.SMEM)
VMEM = pl.BlockSpec(memory_space=pltpu.VMEM)
VMEM_LIMIT = 40 << 20
DELTA_LIMIT = 56 << 20
LATE_LIMIT = 40 << 20
HEADS_A = 2


def dot(a, b, dims):
    return lax.dot_general(a, b, dims, preferred_element_type=F32)


def device_index():
    return lax.axis_index("seq")


def own_starts(doc):
    first = device_index() * NB
    starts = [jnp.int32(0)]
    for i in range(1, NB):
        same = doc[first + i] == doc[first + i - 1]
        starts.append(jnp.where(same, starts[-1], jnp.int32(i)))
    return starts


def crossing(doc, distance):
    me = device_index()
    first = me * NB
    key_first = first - NB * distance
    valid = key_first >= 0
    near = jnp.maximum(key_first, 0)
    keys = jnp.int32(0)
    rows = jnp.int32(0)
    for j in range(NB):
        keys += jnp.where(doc[near + j] == doc[first], 1, 0)
        rows += jnp.where(doc[first + j] == doc[near + NB - 1], 1, 0)
    return jnp.where(valid, keys, 0), jnp.where(valid, rows, 0)


def cols(h):
    if isinstance(h, int):
        return slice(h * DH, (h + 1) * DH)
    return pl.ds(pl.multiple_of(h * DH, DH), DH)


def row(h):
    return pl.ds(h, 1)


def piece(k, v, k_t, q, g, lnorm, delta, bias):
    s = dot(k, q, NT) * (SCALE * LOG2E) - lnorm
    if bias is not None:
        s = s + bias
    p = jnp.exp2(s)
    ds = (p * (dot(v, g, NT) - delta)).astype(BF16)
    dv = dot(p.astype(BF16), g, NN)
    dk = dot(ds, q, NN)
    dq_t = dot(k_t, ds, NN)
    return dq_t, dk, dv


def fill_bias(doc, bias):
    starts = own_starts(doc)
    key = lax.broadcasted_iota(jnp.int32, (TOK, BLK), 0)
    for i in range(NB):
        tok = lax.broadcasted_iota(jnp.int32, (TOK, BLK), 1) + i * BLK
        ok = (key <= tok) & (key >= starts[i] * BLK)
        bias[:, i * BLK : (i + 1) * BLK] = jnp.where(ok, 0.0, FAR).astype(F32)


def own_head(q, g, k, v, k_t, ln, delta, bias, dkv):
    low = slice(0, HALF)
    high = slice(HALF, TOK)
    x0, dk0, dv0 = piece(k[low, :], v[low, :], k_t[:, low], q, g, ln, delta, bias[low, :])
    x1, dk1, dv1 = piece(
        k[high, :], v[high, :], k_t[:, high], q[high, :], g[high, :], ln[:, high], delta[:, high], bias[high, high]
    )
    for rows, dk, dv in ((low, dk0, dv0), (high, dk1, dv1)):
        dkv[rows, 0:DH] += dk
        dkv[rows, DH:] += dv
    return x0[:, low], x0[:, high] + x1


def delta_kernel(doc, a_hbm, g_hbm, delta_out, need_out, g, a, delta, sem_g, sem_a, sem_s):
    def copy_g(n):
        return pltpu.make_async_copy(g_hbm.at[pl.ds(n * BLK, BLK), :], g.at[n], sem_g.at[n])

    def copy_a(n):
        return pltpu.make_async_copy(a_hbm.at[pl.ds(n * BLK, BLK), :], a.at[n], sem_a.at[n])

    for n in range(NB):
        copy_g(n).start()
        copy_a(n).start()
    need = jnp.int32(0)
    for d in range(2, doc.shape[0] // NB):
        need = jnp.where(doc[d * NB] == doc[d * NB - NB - 1], 1, need)
    need_out[0] = need
    lane_head = lax.broadcasted_iota(jnp.int32, (H, H * DH), 1) // DH
    pick = (lane_head == lax.broadcasted_iota(jnp.int32, (H, H * DH), 0)).astype(F32).astype(BF16)
    for n in range(NB):
        copy_g(n).wait()
        copy_a(n).wait()
        prod = g[n].astype(F32) * a[n].astype(F32)
        top = prod.astype(BF16)
        rest = (prod - top.astype(F32)).astype(BF16)
        delta[:, n * BLK : (n + 1) * BLK] = dot(pick, top, NT) + dot(pick, rest, NT)

    c = pltpu.make_async_copy(delta, delta_out, sem_s.at[0])
    c.start()
    c.wait()


def head_deltas(doc, a, g):
    big = pltpu.VMEM((NB, BLK, H * DH), BF16)
    return pl.pallas_call(
        delta_kernel,
        name="delta",
        out_shape=(jax.ShapeDtypeStruct((H, TOK), F32), jax.ShapeDtypeStruct((1,), jnp.int32)),
        in_specs=[SMEM, ANY, ANY],
        out_specs=(ANY, SMEM),
        scratch_shapes=[
            big, big,
            pltpu.VMEM((H, TOK), F32),
            pltpu.SemaphoreType.DMA((NB,)),
            pltpu.SemaphoreType.DMA((NB,)),
            pltpu.SemaphoreType.DMA((1,)),
        ],
        compiler_params=pltpu.CompilerParams(vmem_limit_bytes=DELTA_LIMIT),
        cost_estimate=pl.CostEstimate(flops=4_000_000, bytes_accessed=2_000_000, transcendentals=0),
    )(doc, a, g)


def early_kernel(doc, q, k, v, g, ln, delta, dq_t, dkv, k_t, bias):
    fill_bias(doc, bias)
    k_t[...] = jnp.transpose(k[...])
    dkv[...] = jnp.zeros((TOK, 2 * DH), F32)

    @pl.loop(0, HEADS_A, unroll=2)
    def _(h):
        lo, hi = own_head(
            q[:, cols(h)], g[:, cols(h)], k, v, k_t, ln[row(h), :] * LOG2E, delta[row(h), :], bias, dkv
        )
        dq_t[h, :, 0:HALF] = lo
        dq_t[h, :, HALF:] = hi


def early(doc, q, k, v, g, ln_t, delta):
    return pl.pallas_call(
        early_kernel,
        name="early",
        out_shape=(
            jax.ShapeDtypeStruct((HEADS_A, DH, TOK), F32),
            jax.ShapeDtypeStruct((TOK, 2 * DH), F32),
        ),
        in_specs=[SMEM] + [VMEM] * 6,
        out_specs=(VMEM, VMEM),
        scratch_shapes=[
            pltpu.VMEM((DH, TOK), BF16),
            pltpu.VMEM((TOK, TOK), F32),
        ],
        compiler_params=pltpu.CompilerParams(vmem_limit_bytes=VMEM_LIMIT),
        cost_estimate=pl.CostEstimate(flops=4_000_000_000, bytes_accessed=6_000_000, transcendentals=1_600_000),
    )(doc, q, k, v, g, ln_t, delta)


def dead_rows(ln, n_rows, toks):
    tok_live = lax.broadcasted_iota(jnp.int32, (H, toks), 1) < n_rows * BLK
    return jnp.where(tok_live, ln[:, 0:toks] * LOG2E, -FAR)


def load_keys(k_in, keys, count, k, k_t, acc):
    key_row = lax.broadcasted_iota(jnp.int32, (keys, DH), 0)
    live = key_row >= keys - count * BLK
    k[0:keys, :] = jnp.where(live, k_in[TOK - keys :, :], jnp.zeros((keys, DH), BF16))
    k_t[:, 0:keys] = jnp.transpose(k[0:keys, :])
    acc[0:keys, :] = jnp.zeros((keys, 2 * DH), F32)
    return live


def remote_head(h, q, g, v_in, ln2, delta, k, k_t, acc, keys, toks):
    x, dk, dv = piece(
        k[0:keys, :], v_in[TOK - keys :, :], k_t[:, 0:keys], q[0:toks, cols(h)], g[0:toks, cols(h)],
        ln2[row(h), 0:toks], delta[row(h), 0:toks], None,
    )
    acc[0:keys, 0:DH] += dk
    acc[0:keys, DH:] += dv
    return x


def store_keys(out, acc, keys, live):
    zero = jnp.zeros((keys, DH), F32)
    here = slice(TOK - keys, TOK)
    out[here, 0:DH] = jnp.where(live, acc[0:keys, 0:DH] * SCALE, zero).astype(BF16)
    out[here, DH:] = jnp.where(live, acc[0:keys, DH:], zero).astype(BF16)
    if keys < TOK:
        out[0 : TOK - keys, :] = jnp.zeros((TOK - keys, 2 * DH), BF16)


def near_kernel(doc, q, g, ln, delta, k_in, v_in, dq_t, near, k, k_t, ln2, acc):
    n_keys, n_rows = crossing(doc, 1)

    def run(keys, toks):
        live = load_keys(k_in, keys, n_keys, k, k_t, acc)
        ln2[:, 0:toks] = dead_rows(ln, n_rows, toks)

        @pl.loop(0, H, unroll=4)
        def _(h):
            dq_t[h, :, 0:toks] = remote_head(h, q, g, v_in, ln2, delta, k, k_t, acc, keys, toks)

        store_keys(near, acc, keys, live)

    few_keys = n_keys * BLK <= HALF
    few_rows = n_rows * BLK <= HALF

    @pl.when(n_keys == 0)
    def _():
        near[...] = jnp.zeros((TOK, 2 * DH), BF16)

    for keys in (HALF, TOK):
        for toks in (HALF, TOK):
            ok = (n_keys > 0) & (few_keys == (keys == HALF)) & (few_rows == (toks == HALF))
            pl.when(ok)(functools.partial(run, keys, toks))


def remote_scratch():
    return [
        pltpu.VMEM((TOK, DH), BF16),
        pltpu.VMEM((DH, TOK), BF16),
        pltpu.VMEM((H, TOK), F32),
        pltpu.VMEM((TOK, 2 * DH), F32),
    ]


def near_pieces(doc, q, g, ln_t, delta, k1, v1):
    return pl.pallas_call(
        near_kernel,
        name="near",
        out_shape=(
            jax.ShapeDtypeStruct((H, DH, TOK), F32),
            jax.ShapeDtypeStruct((TOK, 2 * DH), BF16),
        ),
        in_specs=[SMEM] + [VMEM] * 6,
        out_specs=(VMEM, VMEM),
        scratch_shapes=remote_scratch(),
        compiler_params=pltpu.CompilerParams(vmem_limit_bytes=VMEM_LIMIT),
        cost_estimate=pl.CostEstimate(flops=4_000_000_000, bytes_accessed=6_000_000, transcendentals=2_000_000),
    )(doc, q, g, ln_t, delta, k1, v1)


def far_kernel(
    doc, q, g, ln, delta, k_in, v_in,
    dq_out, far,
    k, k_t, ln2, acc,
):
    n_keys, n_rows = crossing(doc, 2)
    dq_out[...] = jnp.zeros((TOK, H * DH), F32)
    far[...] = jnp.zeros((TOK, 2 * DH), BF16)

    @pl.when(n_keys > 0)
    def _():
        live = load_keys(k_in, TOK, n_keys, k, k_t, acc)
        ln2[...] = dead_rows(ln, n_rows, TOK)

        @pl.loop(0, H)
        def _(h):
            x = remote_head(h, q, g, v_in, ln2, delta, k, k_t, acc, TOK, TOK)
            dq_out[:, cols(h)] = jnp.transpose(x) * SCALE

        store_keys(far, acc, TOK, live)


def far_pieces(doc, q, g, ln_t, delta, k2, v2):
    return pl.pallas_call(
        far_kernel,
        name="far",
        out_shape=(
            jax.ShapeDtypeStruct((TOK, H * DH), F32),
            jax.ShapeDtypeStruct((TOK, 2 * DH), BF16),
        ),
        in_specs=[SMEM] + [VMEM] * 6,
        out_specs=(VMEM, VMEM),
        scratch_shapes=remote_scratch(),
        compiler_params=pltpu.CompilerParams(vmem_limit_bytes=VMEM_LIMIT),
        cost_estimate=pl.CostEstimate(flops=4_000_000_000, bytes_accessed=6_000_000, transcendentals=2_000_000),
    )(doc, q, g, ln_t, delta, k2, v2)


def late_kernel(doc, q, k, v, g, ln, delta, own_a, rem, dq, dkv, k_t, bias):
    _, n_rows = crossing(doc, 1)
    fill_bias(doc, bias)
    k_t[...] = jnp.transpose(k[...])
    dkv[...] = jnp.zeros((TOK, 2 * DH), F32)

    def finish(h, own):
        live = lax.broadcasted_iota(jnp.int32, (DH, TOK), 1) < n_rows * BLK
        full = own + jnp.where(live, rem[h], 0.0)
        dq[:, cols(h)] = (jnp.transpose(full) * SCALE).astype(BF16)

    for h in range(HEADS_A):
        finish(h, own_a[h])

    @pl.loop(HEADS_A, H, unroll=3)
    def _(h):
        lo, hi = own_head(
            q[:, cols(h)], g[:, cols(h)], k, v, k_t, ln[row(h), :] * LOG2E, delta[row(h), :], bias, dkv
        )
        finish(h, jnp.concatenate([lo, hi], axis=1))


def late(doc, q, k, v, g, ln_t, delta, own, rem):
    return pl.pallas_call(
        late_kernel,
        name="late",
        out_shape=(
            jax.ShapeDtypeStruct((TOK, H * DH), BF16),
            jax.ShapeDtypeStruct((TOK, 2 * DH), F32),
        ),
        in_specs=[SMEM] + [VMEM] * 8,
        out_specs=(VMEM, VMEM),
        scratch_shapes=[
            pltpu.VMEM((DH, TOK), BF16),
            pltpu.VMEM((TOK, TOK), F32),
        ],
        compiler_params=pltpu.CompilerParams(vmem_limit_bytes=LATE_LIMIT),
        cost_estimate=pl.CostEstimate(flops=4_000_000_000, bytes_accessed=5_000_000, transcendentals=0),
    )(doc, q, k, v, g, ln_t, delta, own, rem)


def moved(value, by):
    count = lax.axis_size("seq")
    return lax.ppermute(value, "seq", [(i, (i + by) % count) for i in range(count)])


def local(queries, key_input, value_input, attn_out, out_grad, log_norm, doc_block):
    ln_t = log_norm.T
    near_k = moved(key_input, 1)
    near_v = moved(value_input, 1)
    delta, need = head_deltas(doc_block, attn_out, out_grad)
    dqt, dkv_a = early(doc_block, queries, key_input, value_input, out_grad, ln_t, delta)
    rem, part = near_pieces(doc_block, queries, out_grad, ln_t, delta, near_k, near_v)
    back = moved(part, -1)
    dq, dkv_b = late(doc_block, queries, key_input, value_input, out_grad, ln_t, delta, dqt, rem)
    dkv = dkv_a + dkv_b
    dk = dkv[:, :DH] * SCALE + back[:, :DH].astype(F32)
    dv = dkv[:, DH:] + back[:, DH:].astype(F32)

    def far_step(_, grads):
        far_k, far_v, grads = lax.optimization_barrier((key_input, value_input, grads))
        far_k = moved(far_k, 2)
        far_v = moved(far_v, 2)
        dq_far, far_part = far_pieces(doc_block, queries, out_grad, ln_t, delta, far_k, far_v)
        far_back = moved(far_part, -2).astype(F32)
        adds = (dq_far, far_back[:, :DH], far_back[:, DH:])
        return tuple((x.astype(F32) + y).astype(BF16) for x, y in zip(grads, adds))

    return lax.fori_loop(0, need[0], far_step, (dq, dk.astype(BF16), dv.astype(BF16)))


def solution(mesh):
    return jax.shard_map(
        local,
        mesh=mesh,
        in_specs=(
            P(("dp", "seq"), None),
            P(("dp", "seq"), None),
            P(("dp", "seq"), None),
            P(("dp", "seq"), None),
            P(("dp", "seq"), None),
            P(("dp", "seq"), None),
            P("dp"),
        ),
        out_specs=(P(("dp", "seq"), None), P(("dp", "seq"), None), P(("dp", "seq"), None)),
        check_vma=False,
    )
```
